512 devices in a mesh: ctx: 64 (over z, x, core), head: 8 (over y).
Axes of the slice: x: 4, y: 8, z: 8, core: 2. Of those that a mesh axis runs over, the one named last changes fastest.
Arguments:
- queries: bfloat16 [24576, 64, 128], P(('ctx', 'head')), may hold values from -6 to 6
- keys: bfloat16 [24576, 64, 128], P(('ctx', 'head')), may hold values from -6 to 6
- values: bfloat16 [24576, 64, 128], P(('ctx', 'head')), may hold values from -6 to 6
- decay_log: bfloat16 [24576, 64], P(('ctx', 'head')), may hold values from -1 to 0, as said below
- out_gain: float32 [64, 128], replicated, may hold values from 0.1 to 1.9
Outputs:
- normed: bfloat16 [24576, 64, 128], P(('ctx', 'head'))
The draws below stay inside these ranges and needn't reach their ends.
Inputs may be any that keep to these rules, and one draw needn't show every extreme that they name: `decay_log`: every entry is negative or zero.
All inputs are finite; a program needn't handle non-finite values.
Results may differ from the reference program's by a relative error of at most 0.01.
Values may be sent and summed in bfloat16 or wider, within the bound.
No kernel may reach another device: no remote copies, remote signals or barrier semaphores. Data moves between devices by JAX's collectives and lax.ppermute only.
A program may use at most 128 MiB of HBM per device.

```python
import jax
import jax.numpy as jnp
from jax import lax

HEAD_COUNT = 64
DH = 128
SEGMENT_TOKENS = 384
TOKEN_COUNT = 24576
N_CTX = 64


def correlated_pair(key):
    shared_key = jax.random.fold_in(key, 101)
    private_key = jax.random.fold_in(key, 202)
    full_shape = (TOKEN_COUNT, HEAD_COUNT, DH)
    shared = jax.random.normal(shared_key, full_shape, jnp.float32)
    private = jax.random.normal(private_key, full_shape, jnp.float32)
    keys_drawn = jnp.clip(shared, -6.0, 6.0)
    values_drawn = jnp.clip(0.8 * shared + 0.6 * private, -6.0, 6.0)
    return (keys_drawn, values_drawn)


def draw_keys(key, part):
    return correlated_pair(key)[0].astype(jnp.bfloat16)


def draw_values(key, part):
    return correlated_pair(key)[1].astype(jnp.bfloat16)


def draw_decay_log(key, part):
    complete_key_rows = jax.random.split(key, 7)
    order = jax.random.permutation(complete_key_rows[0], HEAD_COUNT)
    fast_count = HEAD_COUNT // 2
    rapid_decay = order < fast_count
    fast_rate = jnp.exp(jax.random.uniform(complete_key_rows[1], (HEAD_COUNT,), jnp.float32, jnp.log(1.0 / 50.0), jnp.log(1.0 / 30.0)))
    slow_rate = jnp.exp(jax.random.uniform(complete_key_rows[2], (HEAD_COUNT,), jnp.float32, jnp.log(0.05 / TOKEN_COUNT), jnp.log(0.5 / TOKEN_COUNT)))
    spike_rate = jnp.where(rapid_decay, fast_rate, slow_rate)
    random_offset = jax.random.uniform(complete_key_rows[3], (TOKEN_COUNT, HEAD_COUNT), jnp.float32, 0.5, 1.5)
    spike_position = jax.random.randint(complete_key_rows[4], (4, HEAD_COUNT), 0, TOKEN_COUNT)
    spike_retain = jax.random.uniform(complete_key_rows[5], (4, HEAD_COUNT), jnp.float32, 0.5, 0.8)
    token_position_index = jnp.arange(TOKEN_COUNT, dtype=jnp.int32)
    spike_flags = token_position_index[:, None, None] == spike_position[None, :, :]
    spike_logarithm = jnp.sum(jnp.where(spike_flags, jnp.log(spike_retain)[None], 0.0), axis=1)
    layer_output = jnp.maximum(-spike_rate[None, :] * random_offset + spike_logarithm, -1.0)
    spike_block_index = jax.random.randint(complete_key_rows[6], (), N_CTX - N_CTX // 4, N_CTX - 1)
    spike_first_token = spike_block_index * SEGMENT_TOKENS + SEGMENT_TOKENS - 6
    spike_token_offset = token_position_index - spike_first_token
    spike_marker_mask = (spike_token_offset >= 0) & (spike_token_offset < 6)
    strong_decay_mask = spike_marker_mask[:, None] & jnp.logical_not(rapid_decay)[None, :]
    layer_output = jnp.where(strong_decay_mask, -0.85, layer_output)
    return layer_output.astype(jnp.bfloat16)


def steps_of(stream_key, extent, shards, low, top_value):
    level = 1.0
    for axis_at, parts in shards:
        heights = jax.random.uniform(jax.random.fold_in(jax.random.fold_in(stream_key, 6), axis_at), (parts,), jnp.float32, low / len(shards), top_value / len(shards))
        level = level * jnp.repeat(jnp.exp(heights), extent[axis_at] // parts).reshape((-1,) + (1,) * (len(extent) - 1 - axis_at))
    return level


def gaussian(own_key, shape, scale, limit, cuts=(), held_as=jnp.bfloat16):
    gain = steps_of(own_key, shape, cuts, -0.22, 0.18) if cuts else 1.0
    values = jax.random.normal(own_key, shape, jnp.float32) * scale * gain
    return jnp.minimum(jnp.maximum(values, -limit), limit).astype(held_as)


def setup_inputs(seed: int = 0) -> dict:
    splits = jax.random.split(jax.random.key(seed), 6)
    queries = gaussian(splits[0], (TOKEN_COUNT, HEAD_COUNT, DH), 1.0, 6.0, ((0, 512),))
    keys = draw_keys(jax.random.fold_in(splits[5], 71), 0)
    values = draw_values(jax.random.fold_in(splits[5], 71), 0)
    decay_log = draw_decay_log(jax.random.fold_in(splits[5], 71), 0)
    out_gain = jnp.clip(1.0 + 0.18 * jax.random.normal(splits[4], (HEAD_COUNT, DH), jnp.float32), 0.1, 1.9)
    return {"queries": queries, "keys": keys, "values": values, "decay_log": decay_log, "out_gain": out_gain}


def activate(block):
    return jax.nn.silu(block.astype(jnp.float32)).astype(jnp.bfloat16)

def normalize(mixed, out_gain):
    values32 = mixed.astype(jnp.float32)
    meansq = lax.optimization_barrier(jnp.mean(values32 * values32, axis=(1, 2), keepdims=True))
    return (values32 * lax.rsqrt(meansq + 1e-06) * out_gain[None]).astype(jnp.bfloat16)

def make_step(out_gain):

    def span_step(state, pieces):
        queries_c, keys_c, values_c, decay_c = pieces
        query_act = activate(queries_c).astype(jnp.float32)
        key_act = activate(keys_c).astype(jnp.float32)
        value_act = activate(values_c).astype(jnp.float32)
        cumulative = jnp.cumsum(decay_c.astype(jnp.float32), axis=0)
        length = cumulative.shape[0]
        token_position_index = jnp.arange(length, dtype=jnp.int32)
        causal = (token_position_index[:, None] >= token_position_index[None, :])[None]
        scores = jnp.einsum('thd,shd->hts', query_act, key_act)
        offsets = cumulative.T[:, :, None] - cumulative.T[:, None, :]
        weights = jnp.where(causal, scores * jnp.exp(jnp.where(causal, offsets, -1e+30)), 0.0)
        weights = weights.astype(jnp.bfloat16).astype(jnp.float32)
        intra_out = jnp.einsum('hts,shd->thd', weights, value_act)
        ending = cumulative[-1]
        scaled_keys = (key_act * jnp.exp(ending[None, :] - cumulative)[:, :, None]).astype(jnp.bfloat16)
        local_state = jnp.einsum('shd,she->hde', scaled_keys.astype(jnp.float32), value_act)
        incoming_low = state.astype(jnp.bfloat16).astype(jnp.float32)
        inter_out = jnp.einsum('thd,hde->the', query_act, incoming_low) * jnp.exp(cumulative)[:, :, None]
        mixed = (intra_out + inter_out).astype(jnp.bfloat16)
        new_state = jnp.exp(ending)[:, None, None] * state + local_state
        return (new_state, normalize(mixed, out_gain))
    return span_step

def reference(queries, keys, values, decay_log, out_gain):
    blocked = (queries.reshape(N_CTX, SEGMENT_TOKENS, HEAD_COUNT, DH), keys.reshape(N_CTX, SEGMENT_TOKENS, HEAD_COUNT, DH), values.reshape(N_CTX, SEGMENT_TOKENS, HEAD_COUNT, DH), decay_log.reshape(N_CTX, SEGMENT_TOKENS, HEAD_COUNT))
    start = jnp.zeros((HEAD_COUNT, DH, DH), jnp.float32)
    final_state, normed = lax.scan(make_step(out_gain), start, blocked)
    return normed.reshape(TOKEN_COUNT, HEAD_COUNT, DH)
```

```python
import functools

import jax
import jax.numpy as jnp
from jax import lax
from jax.experimental import pallas as pl
from jax.experimental.pallas import tpu as pltpu
from jax.sharding import Mesh
from jax.sharding import PartitionSpec as P

F32 = jnp.float32
BF16 = jnp.bfloat16
EXTRA = 8
LIMIT = 48 * 1024 * 1024


def iota(shape, axis):
    return lax.broadcasted_iota(jnp.int32, shape, axis)


def silu(x):
    half = 0.5 * x
    return half + half * jnp.tanh(half)


def three_parts(x):
    high = x.astype(BF16)
    rest = x - high.astype(F32)
    middle = rest.astype(BF16)
    low = (rest - middle.astype(F32)).astype(BF16)
    return high, middle, low


def dot_parts(mask, parts):
    return sum(jnp.dot(mask, part, preferred_element_type=F32) for part in parts)


def local_cumulative(decay, group):
    tokens, heads = decay.shape
    tril = (iota((tokens, tokens), 0) >= iota((tokens, tokens), 1)).astype(F32).astype(BF16)
    running = jnp.dot(tril, decay, preferred_element_type=F32)
    wide = jnp.concatenate([running, jnp.zeros((tokens, 128 - heads), F32)], axis=1)
    return pltpu.roll(wide, lax.rem(128 - 8 * group, 128), 1)


def pack_kv_kernel(decay_ref, keys_ref, values_ref, out_ref, key_rows, value_rows):
    tokens = keys_ref.shape[0]
    running = local_cumulative(decay_ref[...], pl.program_id(0))
    key_rows[...] = keys_ref[...].astype(F32).reshape(tokens * 8, 128)
    value_rows[...] = values_ref[...].astype(F32).reshape(tokens * 8, 128)
    to_end = jnp.exp(running[tokens - 1 : tokens, :] - running)
    row = iota((EXTRA, 128), 0)
    for j in range(8):
        rows = pl.ds(j, tokens, stride=8)
        scale = jnp.broadcast_to(to_end[:, j : j + 1], (tokens, 128))
        out_ref[j, 0:tokens, :] = (silu(key_rows[rows, :]) * scale).astype(BF16)
        out_ref[j, tokens : 2 * tokens, :] = silu(value_rows[rows, :]).astype(BF16)
        total = jnp.broadcast_to(running[tokens - 1 : tokens, j : j + 1], (EXTRA, 128))
        high, middle, low = (part.astype(F32) for part in three_parts(total))
        out_ref[j, 2 * tokens : 2 * tokens + EXTRA, :] = jnp.where(
            row == 0, high, jnp.where(row == 1, middle, jnp.where(row == 2, low, 0.0))
        ).astype(BF16)


def pack_kv(keys, values, decay):
    tokens, heads, dim = keys.shape
    block = pl.BlockSpec((tokens, 8, dim), lambda g: (0, g, 0))
    return pl.pallas_call(
        pack_kv_kernel,
        grid=(heads // 8,),
        in_specs=[pl.BlockSpec((tokens, heads), lambda g: (0, 0)), block, block],
        out_specs=pl.BlockSpec((8, 2 * tokens + EXTRA, dim), lambda g: (g, 0, 0)),
        out_shape=jax.ShapeDtypeStruct((heads, 2 * tokens + EXTRA, dim), BF16),
        scratch_shapes=[pltpu.VMEM((tokens * 8, dim), F32)] * 2,
        compiler_params=pltpu.CompilerParams(vmem_limit_bytes=LIMIT),
        name="pack_kv",
    )(decay, keys, values)


def pack_q_kernel(decay_ref, queries_ref, out_ref, query_rows):
    tokens = queries_ref.shape[0]
    running = local_cumulative(decay_ref[...], pl.program_id(0))
    query_rows[...] = queries_ref[...].astype(F32).reshape(tokens * 8, 128)
    grown = jnp.exp(running)
    for j in range(8):
        scale = jnp.broadcast_to(grown[:, j : j + 1], (tokens, 128))
        rows = query_rows[pl.ds(j, tokens, stride=8), :]
        out_ref[j] = (silu(rows) * scale).astype(BF16)


def pack_q(queries, decay):
    tokens, heads, dim = queries.shape
    return pl.pallas_call(
        pack_q_kernel,
        grid=(heads // 8,),
        in_specs=[
            pl.BlockSpec((tokens, heads), lambda g: (0, 0)),
            pl.BlockSpec((tokens, 8, dim), lambda g: (0, g, 0)),
        ],
        out_specs=pl.BlockSpec((8, tokens, dim), lambda g: (g, 0, 0)),
        out_shape=jax.ShapeDtypeStruct((heads, tokens, dim), BF16),
        scratch_shapes=[pltpu.VMEM((tokens * 8, dim), F32)],
        compiler_params=pltpu.CompilerParams(vmem_limit_bytes=LIMIT),
        name="pack_q",
    )(decay, queries)


def states_kernel(per_block, kv_ref, prefix_ref, total_ref, factor_ref, enter_ref, reach_ref):
    sources, rows, dim = kv_ref.shape
    tokens = (rows - EXTRA) // 2
    blocks = sources // per_block
    length = per_block * tokens
    tail = kv_ref[:, 2 * tokens : rows, :].astype(F32)
    totals = jnp.sum(tail, axis=1)
    parts = three_parts(totals)
    at, of = iota((sources, sources), 0), iota((sources, sources), 1)
    same = at // per_block == of // per_block

    def mask(keep):
        return keep.astype(F32).astype(BF16)

    before = dot_parts(mask(same & (of < at)), parts)
    after = dot_parts(mask(same & (of > at)), parts)
    enter_ref[...] = jnp.exp(before)
    to_block_end = jnp.exp(after)
    block_at, source_of = iota((blocks, sources), 0), iota((blocks, sources), 1) // per_block
    block_total = dot_parts(mask(block_at == source_of), parts)
    block_before = dot_parts(mask(block_at > source_of), parts)
    reach_ref[...] = jnp.exp(block_before)
    in_lanes = jnp.transpose(totals)[0:blocks, :]
    picked = jnp.where(block_at == source_of, in_lanes, 0.0)
    member, position = iota((sources, length), 0), iota((sources, length), 1)
    up_to = mask(lax.rem(member, per_block) <= position // tokens)
    through = sum(jnp.dot(part, up_to, preferred_element_type=F32) for part in three_parts(picked))
    source_row = iota((per_block, length), 0)
    source_col = iota((per_block, length), 1) // tokens
    repeats = length // dim
    state = jnp.zeros((dim, dim), F32)
    for b in range(blocks):
        here = slice(b * per_block, (b + 1) * per_block)
        start = jnp.concatenate([before[here]] * repeats, axis=1)
        factor_ref[b] = jnp.where(
            source_col <= source_row, jnp.exp(start - through[b : b + 1, :]), 0.0
        )
        prefix_ref[b] = state
        keys = kv_ref[here, 0:tokens, :].astype(F32) * to_block_end[here][:, None, :]
        values = kv_ref[here, tokens : 2 * tokens, :].reshape(length, dim)
        own = lax.dot_general(
            keys.astype(BF16).reshape(length, dim), values, (((0,), (0,)), ((), ())),
            preferred_element_type=F32,
        )
        state = jnp.exp(block_total[b : b + 1, :]) * state + own
    total_ref[0:dim, :] = state
    total_ref[dim : dim + 8, :] = jnp.broadcast_to(
        jnp.sum(block_total, axis=0, keepdims=True), (8, dim)
    )


def states(kv, per_block):
    sources, rows, dim = kv.shape
    blocks, length = sources // per_block, per_block * (rows - EXTRA) // 2
    return pl.pallas_call(
        functools.partial(states_kernel, per_block),
        out_shape=(
            jax.ShapeDtypeStruct((blocks, dim, dim), F32),
            jax.ShapeDtypeStruct((dim + 8, dim), F32),
            jax.ShapeDtypeStruct((blocks, per_block, length), F32),
            jax.ShapeDtypeStruct((sources, dim), F32),
            jax.ShapeDtypeStruct((blocks, dim), F32),
        ),
        compiler_params=pltpu.CompilerParams(vmem_limit_bytes=LIMIT),
        name="states",
    )(kv)


def attend_kernel(query_ref, kv_ref, prefix_ref, factor_ref, enter_ref, reach_ref, incoming_ref, out_ref):
    per_block, tokens, dim = query_ref.shape
    length = per_block * tokens
    b = pl.program_id(0)
    query = query_ref[...].reshape(length, dim)
    key = kv_ref[:, 0:tokens, :].reshape(length, dim)
    value = kv_ref[:, tokens : 2 * tokens, :].reshape(length, dim)
    state = prefix_ref[0] + reach_ref[pl.ds(b, 1), :] * incoming_ref[...]
    inter = jnp.dot(query, state.astype(BF16), preferred_element_type=F32)

    def spread(x):
        return jnp.concatenate(
            [jnp.broadcast_to(x[i : i + 1], (tokens, x.shape[1])) for i in range(per_block)], axis=0
        )

    factor = spread(factor_ref[0])
    enter = spread(enter_ref[...])
    step = 128
    causal = iota((step, step), 0) >= iota((step, step), 1)
    for low in range(0, length, step):
        high = low + step
        scores = lax.dot_general(
            query[low:high], key[0:high], (((1,), (1,)), ((), ())), preferred_element_type=F32
        )
        scores = scores * factor[low:high, 0:high]
        diagonal = jnp.where(causal, scores[:, low:high], 0.0)
        if low:
            scores = jnp.concatenate([scores[:, 0:low], diagonal], axis=1)
        else:
            scores = diagonal
        intra = jnp.dot(scores.astype(BF16), value[0:high], preferred_element_type=F32)
        mixed = (intra + enter[low:high] * inter[low:high]).astype(BF16)
        for i in range(low // 16, high // 16):
            source, row = divmod(i * 16, tokens)
            out_ref[source, row : row + 16, :] = mixed[i * 16 - low : i * 16 - low + 16]


def attend(query, kv, prefix, factor, enter, reach, incoming, per_block):
    sources, tokens, dim = query.shape
    rows = kv.shape[1]
    blocks, length = sources // per_block, per_block * tokens

    def whole(shape):
        return pl.BlockSpec(shape, lambda b: (0,) * len(shape))

    return pl.pallas_call(
        attend_kernel,
        grid=(blocks,),
        in_specs=[
            pl.BlockSpec((per_block, tokens, dim), lambda b: (b, 0, 0)),
            pl.BlockSpec((per_block, rows, dim), lambda b: (b, 0, 0)),
            pl.BlockSpec((1, dim, dim), lambda b: (b, 0, 0)),
            pl.BlockSpec((1, per_block, length), lambda b: (b, 0, 0)),
            pl.BlockSpec((per_block, dim), lambda b: (b, 0)),
            whole((blocks, dim)),
            whole((dim, dim)),
        ],
        out_specs=pl.BlockSpec((per_block, tokens, dim), lambda b: (b, 0, 0)),
        out_shape=jax.ShapeDtypeStruct((sources, tokens, dim), BF16),
        compiler_params=pltpu.CompilerParams(vmem_limit_bytes=LIMIT),
        name="attend",
    )(query, kv, prefix, factor, enter, reach, incoming)


def norm_kernel(mixed_ref, gain_ref, out_ref, rows_ref):
    heads, tokens, dim = mixed_ref.shape
    squares = jnp.zeros((tokens, dim), F32)
    for h in range(heads):
        x = mixed_ref[h].astype(F32)
        squares = squares + x * x
    mean = jnp.sum(squares, axis=1, keepdims=True) * (1.0 / (heads * dim))
    scale = jnp.broadcast_to(lax.rsqrt(mean + 1e-06), (tokens, dim))
    for h in range(heads):
        x = mixed_ref[h].astype(F32) * scale * gain_ref[h : h + 1, :]
        rows_ref[pl.ds(h, tokens, stride=heads), :] = x
    for t in range(tokens):
        out_ref[t] = rows_ref[t * heads : (t + 1) * heads, :].astype(BF16)


def norm(mixed, gain):
    heads, tokens, dim = mixed.shape
    return pl.pallas_call(
        norm_kernel,
        out_shape=jax.ShapeDtypeStruct((tokens, heads, dim), BF16),
        scratch_shapes=[pltpu.VMEM((tokens * heads, dim), F32)],
        compiler_params=pltpu.CompilerParams(vmem_limit_bytes=LIMIT),
        name="norm",
    )(mixed, gain)


def incoming_state(own):
    dim = own.shape[1]
    segment = lax.axis_index("seg")
    count = lax.axis_size("seg")
    whole = own
    entering = jnp.zeros_like(own)

    def join(earlier, later):
        decay = jnp.exp(later[dim : dim + 1])
        return jnp.concatenate([decay * earlier[:dim] + later[:dim], earlier[dim:] + later[dim:]], axis=0)

    hop = 1
    while hop < count // 2:
        other = lax.ppermute(whole, "seg", [(i, i ^ hop) for i in range(count)])
        upper = (segment & hop) != 0
        entering = jnp.where(upper, join(other, entering), entering)
        whole = jnp.where(upper, join(other, whole), join(whole, other))
        hop *= 2
    half = count // 2
    other = lax.ppermute(whole, "seg", [(i, half + (i + half // 2) % half) for i in range(half)])
    return jnp.exp(entering[dim : dim + 1]) * other[:dim] + entering[:dim]


def shards(queries, keys, values, decay_log, out_gain):
    per_block = lax.axis_size("head")
    group = ("sub", "head")
    kv = lax.all_to_all(pack_kv(keys, values, decay_log), group, 0, 0, tiled=True)
    query = lax.all_to_all(pack_q(queries, decay_log), group, 0, 0, tiled=True)
    prefix, total, factor, enter, reach = states(kv, per_block)
    incoming = incoming_state(total)
    mixed = attend(query, kv, prefix, factor, enter, reach, incoming, per_block)
    mixed = lax.all_to_all(mixed, group, 0, 0, tiled=True)
    return norm(mixed, out_gain)


def solution(mesh):
    devices = mesh.devices
    contexts, per_block = devices.shape
    heads = 64
    sub = heads // per_block
    split = Mesh(devices.reshape(contexts // sub, sub, per_block), ("seg", "sub", "head"))
    rows = ("seg", "sub", "head")
    return jax.shard_map(
        shards,
        mesh=split,
        in_specs=(P(rows, None, None), P(rows, None, None), P(rows, None, None), P(rows, None), P()),
        out_specs=P(rows, None, None),
        check_vma=False,
    )
```

```python
import functools

import jax
import jax.numpy as jnp
from jax import lax
from jax.experimental import pallas as pl
from jax.experimental.pallas import tpu as pltpu
from jax.sharding import Mesh
from jax.sharding import PartitionSpec as P

F32 = jnp.float32
BF16 = jnp.bfloat16
GROUP = 16
EXTRA = 8
LIMIT = 16 * 1024 * 1024
FULL = 60 * 1024 * 1024


def iota(shape, axis):
    return lax.broadcasted_iota(jnp.int32, shape, axis)


def silu(x):
    half = 0.5 * x
    return half + half * jnp.tanh(half)


def three_parts(x):
    high = x.astype(BF16)
    rest = x - high.astype(F32)
    middle = rest.astype(BF16)
    low = (rest - middle.astype(F32)).astype(BF16)
    return high, middle, low


def dot_parts(mask, parts):
    return sum(jnp.dot(mask, part, preferred_element_type=F32) for part in parts)


def cumulative(decay):
    tokens, heads = decay.shape
    tril = (iota((tokens, tokens), 0) >= iota((tokens, tokens), 1)).astype(F32).astype(BF16)
    running = jnp.dot(tril, decay, preferred_element_type=F32)
    return jnp.concatenate([running, jnp.zeros((tokens, 128 - heads), F32)], axis=1)


def group_lanes(x, head):
    return pltpu.roll(x, lax.rem(128 - head, 128), 1)


def pack_kv_kernel(
    decay_hbm, keys_hbm, values_hbm, out_hbm,
    decay, keys, values, key_rows, value_rows, to_end, totals, out, decay_sem, in_sem, out_sem,
):
    tokens, heads, _ = keys.shape
    groups = heads // GROUP

    def copies_in(g):
        columns = pl.ds(g * GROUP, GROUP)
        return [
            pltpu.make_async_copy(source.at[:, columns, :], target.at[:, columns, :], in_sem.at[i, g])
            for i, (source, target) in enumerate(((keys_hbm, keys), (values_hbm, values)))
        ]

    def copy_out(g):
        here = pl.ds(g * GROUP, GROUP)
        return pltpu.make_async_copy(out.at[here], out_hbm.at[here], out_sem.at[g])

    decay_copy = pltpu.make_async_copy(decay_hbm, decay, decay_sem)
    decay_copy.start()
    for g in range(groups):
        for copy in copies_in(g):
            copy.start()
    decay_copy.wait()
    running = cumulative(decay[...])
    to_end[...] = jnp.exp(running[tokens - 1 : tokens, :] - running)
    row = iota((EXTRA, 128), 0)
    total = jnp.broadcast_to(running[tokens - 1 : tokens, :], (EXTRA, 128))
    high, middle, low = (part.astype(F32) for part in three_parts(total))
    totals[...] = jnp.where(row == 0, high, jnp.where(row == 1, middle, jnp.where(row == 2, low, 0.0)))

    def one(g, carry):
        for copy in copies_in(g):
            copy.wait()
        columns = pl.ds(g * GROUP, GROUP)
        scales, ends = group_lanes(to_end[...], g * GROUP), group_lanes(totals[...], g * GROUP)
        key_rows[...] = keys[:, columns, :].astype(F32).reshape(tokens * GROUP, 128)
        value_rows[...] = values[:, columns, :].astype(F32).reshape(tokens * GROUP, 128)
        for j in range(GROUP):
            rows = pl.ds(j, tokens, stride=GROUP)
            head = g * GROUP + j
            scale = jnp.broadcast_to(scales[:, j : j + 1], (tokens, 128))
            out[head, 0:tokens, :] = (silu(key_rows[rows, :]) * scale).astype(BF16)
            out[head, tokens : 2 * tokens, :] = silu(value_rows[rows, :]).astype(BF16)
            end = jnp.broadcast_to(ends[:, j : j + 1], (EXTRA, 128))
            out[head, 2 * tokens : 2 * tokens + EXTRA, :] = end.astype(BF16)
        copy_out(g).start()
        return carry

    lax.fori_loop(0, groups, one, 0)
    for g in range(groups):
        copy_out(g).wait()


def pack_kv(keys, values, decay):
    tokens, heads, dim = keys.shape
    anywhere = pl.BlockSpec(memory_space=pl.ANY)
    packed = (heads, 2 * tokens + EXTRA, dim)
    return pl.pallas_call(
        pack_kv_kernel,
        in_specs=[anywhere] * 3,
        out_specs=anywhere,
        out_shape=jax.ShapeDtypeStruct(packed, BF16),
        scratch_shapes=[
            pltpu.VMEM(decay.shape, BF16),
            pltpu.VMEM(keys.shape, BF16),
            pltpu.VMEM(values.shape, BF16),
            pltpu.VMEM((tokens * GROUP, dim), F32),
            pltpu.VMEM((tokens * GROUP, dim), F32),
            pltpu.VMEM((tokens, 128), F32),
            pltpu.VMEM((EXTRA, 128), F32),
            pltpu.VMEM(packed, BF16),
            pltpu.SemaphoreType.DMA,
            pltpu.SemaphoreType.DMA((2, heads // GROUP)),
            pltpu.SemaphoreType.DMA((heads // GROUP,)),
        ],
        compiler_params=pltpu.CompilerParams(vmem_limit_bytes=FULL),
        name="pack_kv",
    )(decay, keys, values)


def pack_q_kernel(decay_ref, queries_ref, out_ref, query_rows):
    tokens = queries_ref.shape[0]
    running = group_lanes(cumulative(decay_ref[...]), 8 * pl.program_id(0))
    query_rows[...] = queries_ref[...].astype(F32).reshape(tokens * 8, 128)
    grown = jnp.exp(running)
    for j in range(8):
        scale = jnp.broadcast_to(grown[:, j : j + 1], (tokens, 128))
        rows = query_rows[pl.ds(j, tokens, stride=8), :]
        out_ref[j] = (silu(rows) * scale).astype(BF16)


def pack_q(queries, decay):
    tokens, heads, dim = queries.shape
    return pl.pallas_call(
        pack_q_kernel,
        grid=(heads // 8,),
        in_specs=[
            pl.BlockSpec((tokens, heads), lambda g: (0, 0)),
            pl.BlockSpec((tokens, 8, dim), lambda g: (0, g, 0)),
        ],
        out_specs=pl.BlockSpec((8, tokens, dim), lambda g: (g, 0, 0)),
        out_shape=jax.ShapeDtypeStruct((heads, tokens, dim), BF16),
        scratch_shapes=[pltpu.VMEM((tokens * 8, dim), F32)],
        compiler_params=pltpu.CompilerParams(vmem_limit_bytes=LIMIT),
        name="pack_q",
    )(decay, queries)


def states_kernel(per_block, kv_ref, prefix_ref, total_ref, decay_ref, factor_ref, enter_ref, reach_ref):
    sources, rows, dim = kv_ref.shape
    tokens = (rows - EXTRA) // 2
    blocks = sources // per_block
    length = per_block * tokens
    tail = kv_ref[:, 2 * tokens : rows, :].astype(F32)
    totals = jnp.sum(tail, axis=1)
    parts = three_parts(totals)
    at, of = iota((sources, sources), 0), iota((sources, sources), 1)
    same = at // per_block == of // per_block

    def mask(keep):
        return keep.astype(F32).astype(BF16)

    before = dot_parts(mask(same & (of < at)), parts)
    after = dot_parts(mask(same & (of > at)), parts)
    enter_ref[...] = jnp.exp(before)
    to_block_end = jnp.exp(after)
    block_at, source_of = iota((blocks, sources), 0), iota((blocks, sources), 1) // per_block
    block_total = dot_parts(mask(block_at == source_of), parts)
    block_before = dot_parts(mask(block_at > source_of), parts)
    reach_ref[...] = jnp.exp(block_before)
    in_lanes = jnp.transpose(totals)[0:blocks, :]
    picked = jnp.where(block_at == source_of, in_lanes, 0.0)
    member, position = iota((sources, length), 0), iota((sources, length), 1)
    up_to = mask(lax.rem(member, per_block) <= position // tokens)
    through = sum(jnp.dot(part, up_to, preferred_element_type=F32) for part in three_parts(picked))
    source_row = iota((per_block, length), 0)
    source_col = iota((per_block, length), 1) // tokens
    repeats = length // dim
    state = jnp.zeros((dim, dim), F32)
    for b in range(blocks):
        here = slice(b * per_block, (b + 1) * per_block)
        start = jnp.concatenate([before[here]] * repeats, axis=1)
        factor_ref[b] = jnp.where(
            source_col <= source_row, jnp.exp(start - through[b : b + 1, :]), 0.0
        )
        prefix_ref[b] = state
        keys = kv_ref[here, 0:tokens, :].astype(F32) * to_block_end[here][:, None, :]
        values = kv_ref[here, tokens : 2 * tokens, :].reshape(length, dim)
        own = lax.dot_general(
            keys.astype(BF16).reshape(length, dim), values, (((0,), (0,)), ((), ())),
            preferred_element_type=F32,
        )
        state = jnp.exp(block_total[b : b + 1, :]) * state + own
    total_ref[...] = state
    decay_ref[...] = jnp.exp(jnp.sum(block_total, axis=0, keepdims=True))


def states(kv, per_block):
    sources, rows, dim = kv.shape
    blocks, length = sources // per_block, per_block * (rows - EXTRA) // 2
    return pl.pallas_call(
        functools.partial(states_kernel, per_block),
        out_shape=(
            jax.ShapeDtypeStruct((blocks, dim, dim), F32),
            jax.ShapeDtypeStruct((dim, dim), F32),
            jax.ShapeDtypeStruct((1, dim), F32),
            jax.ShapeDtypeStruct((blocks, per_block, length), F32),
            jax.ShapeDtypeStruct((sources, dim), F32),
            jax.ShapeDtypeStruct((blocks, dim), F32),
        ),
        compiler_params=pltpu.CompilerParams(vmem_limit_bytes=LIMIT),
        name="states",
    )(kv)


def attend_kernel(query_ref, kv_ref, prefix_ref, factor_ref, enter_ref, reach_ref, incoming_ref, out_ref):
    sources, tokens, dim = query_ref.shape
    blocks = prefix_ref.shape[0]
    per_block = sources // blocks
    length = per_block * tokens
    step = 128
    causal = iota((step, step), 0) >= iota((step, step), 1)

    def spread(x):
        return jnp.concatenate(
            [jnp.broadcast_to(x[i : i + 1], (tokens, x.shape[1])) for i in range(per_block)], axis=0
        )

    def weights(b):
        here = slice(b * per_block, (b + 1) * per_block)
        query = query_ref[here].reshape(length, dim)
        key = kv_ref[here, 0:tokens, :].reshape(length, dim)
        factor = spread(factor_ref[b])
        tiles = []
        for low in range(0, length, step):
            high = low + step
            scores = lax.dot_general(
                query[low:high], key[0:high], (((1,), (1,)), ((), ())), preferred_element_type=F32
            )
            scores = scores * factor[low:high, 0:high]
            diagonal = jnp.where(causal, scores[:, low:high], 0.0)
            if low:
                diagonal = jnp.concatenate([scores[:, 0:low], diagonal], axis=1)
            tiles.append(diagonal.astype(BF16))
        return tiles

    def finish(b, tiles):
        here = slice(b * per_block, (b + 1) * per_block)
        query = query_ref[here].reshape(length, dim)
        value = kv_ref[here, tokens : 2 * tokens, :].reshape(length, dim)
        state = prefix_ref[b] + reach_ref[b : b + 1, :] * incoming_ref[...]
        inter = jnp.dot(query, state.astype(BF16), preferred_element_type=F32)
        enter = spread(enter_ref[here])
        for low in range(0, length, step):
            high = low + step
            intra = jnp.dot(tiles[low // step], value[0:high], preferred_element_type=F32)
            mixed = (intra + enter[low:high] * inter[low:high]).astype(BF16)
            for i in range(low // 16, high // 16):
                source, row = divmod(i * 16, tokens)
                piece = mixed[i * 16 - low : i * 16 - low + 16]
                out_ref[b * per_block + source, row : row + 16, :] = piece

    tiles = weights(0)
    for b in range(blocks):
        following = weights(b + 1) if b + 1 < blocks else None
        finish(b, tiles)
        tiles = following


def attend(query, kv, prefix, factor, enter, reach, incoming):
    return pl.pallas_call(
        attend_kernel,
        out_shape=jax.ShapeDtypeStruct(query.shape, BF16),
        compiler_params=pltpu.CompilerParams(vmem_limit_bytes=LIMIT),
        name="attend",
    )(query, kv, prefix, factor, enter, reach, incoming)


def norm_kernel(parts, mixed_ref, gain_ref, out_hbm, rows, out, out_sem):
    heads, tokens, dim = mixed_ref.shape
    squares = [jnp.zeros((tokens, dim), F32) for _ in range(4)]
    for h in range(heads):
        x = mixed_ref[h].astype(F32)
        squares[h % 4] = squares[h % 4] + x * x
    total = squares[0] + squares[1] + squares[2] + squares[3]
    mean = jnp.sum(total, axis=1, keepdims=True) * (1.0 / (heads * dim))
    scale = jnp.broadcast_to(lax.rsqrt(mean + 1e-06), (tokens, dim))
    size = tokens // parts

    def copy_out(p):
        here = pl.ds(p * size, size)
        return pltpu.make_async_copy(out.at[here], out_hbm.at[here], out_sem.at[p])

    for p in range(parts):
        first, last = p * size, (p + 1) * size
        for h in range(heads):
            x = mixed_ref[h, first:last, :].astype(F32) * scale[first:last] * gain_ref[h : h + 1, :]
            rows[pl.ds(first * heads + h, size, stride=heads), :] = x
        for t in range(first, last):
            out[t] = rows[t * heads : (t + 1) * heads, :].astype(BF16)
        copy_out(p).start()
    for p in range(parts):
        copy_out(p).wait()


def norm(mixed, gain):
    heads, tokens, dim = mixed.shape
    parts = 6
    return pl.pallas_call(
        functools.partial(norm_kernel, parts),
        out_specs=pl.BlockSpec(memory_space=pl.ANY),
        out_shape=jax.ShapeDtypeStruct((tokens, heads, dim), BF16),
        scratch_shapes=[
            pltpu.VMEM((tokens * heads, dim), F32),
            pltpu.VMEM((tokens, heads, dim), BF16),
            pltpu.SemaphoreType.DMA((parts,)),
        ],
        compiler_params=pltpu.CompilerParams(vmem_limit_bytes=LIMIT),
        name="norm",
    )(mixed, gain)


def sent(pair):
    state, decay = pair
    high = lax.reduce_precision(decay, 8, 7)
    rows = [state, high, decay - high, jnp.zeros((6, state.shape[1]), F32)]
    return jnp.concatenate([row.astype(BF16) for row in rows], axis=0)


def received(rows):
    dim = rows.shape[1]
    rows = rows.astype(F32)
    return rows[:dim], rows[dim : dim + 1] + rows[dim + 1 : dim + 2]


def join(earlier, later):
    return later[1] * earlier[0] + later[0], earlier[1] * later[1]


def incoming_state(state, decay):
    segment = lax.axis_index("seg")
    count = lax.axis_size("seg")
    whole = (state, decay)
    entering = (jnp.zeros_like(state), jnp.ones_like(decay))
    hop = 1
    while hop < count // 2:
        other = received(lax.ppermute(sent(whole), "seg", [(i, i ^ hop) for i in range(count)]))
        upper = (segment & hop) != 0
        entering = jax.tree.map(lambda a, b: jnp.where(upper, a, b), join(other, entering), entering)
        whole = jax.tree.map(lambda a, b: jnp.where(upper, a, b), join(other, whole), join(whole, other))
        hop *= 2
    half = count // 2
    other = received(lax.ppermute(sent(whole), "seg", [(i, i + half) for i in range(half)]))
    return entering[1] * other[0] + entering[0]


def shards(queries, keys, values, decay_log, out_gain):
    per_block = lax.axis_size("head")
    group = ("sub", "head")
    kv = lax.all_to_all(pack_kv(keys, values, decay_log), group, 0, 0, tiled=True)
    query = lax.all_to_all(pack_q(queries, decay_log), group, 0, 0, tiled=True)
    prefix, total, decay, factor, enter, reach = states(kv, per_block)
    incoming = incoming_state(total, decay)
    mixed = attend(query, kv, prefix, factor, enter, reach, incoming)
    mixed = lax.all_to_all(mixed, group, 0, 0, tiled=True)
    return norm(mixed, out_gain)


def solution(mesh):
    devices = mesh.devices
    contexts, per_block = devices.shape
    heads = 64
    sub = heads // per_block
    split = Mesh(devices.reshape(contexts // sub, sub, per_block), ("seg", "sub", "head"))
    rows = ("seg", "sub", "head")
    return jax.shard_map(
        shards,
        mesh=split,
        in_specs=(P(rows, None, None), P(rows, None, None), P(rows, None, None), P(rows, None), P()),
        out_specs=P(rows, None, None),
        check_vma=False,
    )
```

```python
import functools

import jax
import jax.numpy as jnp
from jax import lax
from jax.experimental import pallas as pl
from jax.experimental.pallas import tpu as pltpu
from jax.sharding import Mesh
from jax.sharding import PartitionSpec as P

F32 = jnp.float32
BF16 = jnp.bfloat16
GROUP = 16
EXTRA = 8
LIMIT = 16 * 1024 * 1024
FULL = 60 * 1024 * 1024


def iota(shape, axis):
    return lax.broadcasted_iota(jnp.int32, shape, axis)


def silu(x):
    half = 0.5 * x
    return half + half * jnp.tanh(half)


def three_parts(x):
    high = x.astype(BF16)
    rest = x - high.astype(F32)
    middle = rest.astype(BF16)
    low = (rest - middle.astype(F32)).astype(BF16)
    return high, middle, low


def dot_parts(mask, parts):
    return sum(jnp.dot(mask, part, preferred_element_type=F32) for part in parts)


def cumulative(decay):
    tokens, heads = decay.shape
    tril = (iota((tokens, tokens), 0) >= iota((tokens, tokens), 1)).astype(F32).astype(BF16)
    running = jnp.dot(tril, decay, preferred_element_type=F32)
    return jnp.concatenate([running, jnp.zeros((tokens, 128 - heads), F32)], axis=1)


def group_lanes(x, head):
    return pltpu.roll(x, lax.rem(128 - head, 128), 1)


def pack_kv_kernel(
    decay_hbm, keys_hbm, values_hbm, out_hbm,
    decay, keys, values, key_rows, value_rows, to_end, totals, out, decay_sem, in_sem, out_sem,
):
    tokens, heads, _ = keys.shape
    groups = heads // GROUP

    def copies_in(g):
        columns = pl.ds(g * GROUP, GROUP)
        return [
            pltpu.make_async_copy(source.at[:, columns, :], target.at[:, columns, :], in_sem.at[i, g])
            for i, (source, target) in enumerate(((keys_hbm, keys), (values_hbm, values)))
        ]

    def copy_out(g):
        here = pl.ds(g * GROUP, GROUP)
        return pltpu.make_async_copy(out.at[here], out_hbm.at[here], out_sem.at[g])

    decay_copy = pltpu.make_async_copy(decay_hbm, decay, decay_sem)
    decay_copy.start()
    for g in range(groups):
        for copy in copies_in(g):
            copy.start()
    decay_copy.wait()
    running = cumulative(decay[...])
    to_end[...] = jnp.exp(running[tokens - 1 : tokens, :] - running)
    row = iota((EXTRA, 128), 0)
    total = jnp.broadcast_to(running[tokens - 1 : tokens, :], (EXTRA, 128))
    high, middle, low = (part.astype(F32) for part in three_parts(total))
    totals[...] = jnp.where(row == 0, high, jnp.where(row == 1, middle, jnp.where(row == 2, low, 0.0)))

    def one(g, carry):
        for copy in copies_in(g):
            copy.wait()
        columns = pl.ds(g * GROUP, GROUP)
        scales, ends = group_lanes(to_end[...], g * GROUP), group_lanes(totals[...], g * GROUP)
        key_rows[...] = keys[:, columns, :].astype(F32).reshape(tokens * GROUP, 128)
        value_rows[...] = values[:, columns, :].astype(F32).reshape(tokens * GROUP, 128)
        for j in range(GROUP):
            rows = pl.ds(j, tokens, stride=GROUP)
            head = g * GROUP + j
            scale = jnp.broadcast_to(scales[:, j : j + 1], (tokens, 128))
            out[head, 0:tokens, :] = (silu(key_rows[rows, :]) * scale).astype(BF16)
            out[head, tokens : 2 * tokens, :] = silu(value_rows[rows, :]).astype(BF16)
            end = jnp.broadcast_to(ends[:, j : j + 1], (EXTRA, 128))
            out[head, 2 * tokens : 2 * tokens + EXTRA, :] = end.astype(BF16)
        copy_out(g).start()
        return carry

    lax.fori_loop(0, groups, one, 0)
    for g in range(groups):
        copy_out(g).wait()


def pack_kv(keys, values, decay):
    tokens, heads, dim = keys.shape
    anywhere = pl.BlockSpec(memory_space=pl.ANY)
    packed = (heads, 2 * tokens + EXTRA, dim)
    return pl.pallas_call(
        pack_kv_kernel,
        in_specs=[anywhere] * 3,
        out_specs=anywhere,
        out_shape=jax.ShapeDtypeStruct(packed, BF16),
        scratch_shapes=[
            pltpu.VMEM(decay.shape, BF16),
            pltpu.VMEM(keys.shape, BF16),
            pltpu.VMEM(values.shape, BF16),
            pltpu.VMEM((tokens * GROUP, dim), F32),
            pltpu.VMEM((tokens * GROUP, dim), F32),
            pltpu.VMEM((tokens, 128), F32),
            pltpu.VMEM((EXTRA, 128), F32),
            pltpu.VMEM(packed, BF16),
            pltpu.SemaphoreType.DMA,
            pltpu.SemaphoreType.DMA((2, heads // GROUP)),
            pltpu.SemaphoreType.DMA((heads // GROUP,)),
        ],
        compiler_params=pltpu.CompilerParams(vmem_limit_bytes=FULL),
        name="pack_kv",
    )(decay, keys, values)


def pack_q_kernel(decay_ref, queries_ref, out_ref, query_rows):
    tokens = queries_ref.shape[0]
    running = group_lanes(cumulative(decay_ref[...]), 8 * pl.program_id(0))
    query_rows[...] = queries_ref[...].astype(F32).reshape(tokens * 8, 128)
    grown = jnp.exp(running)
    for j in range(8):
        scale = jnp.broadcast_to(grown[:, j : j + 1], (tokens, 128))
        rows = query_rows[pl.ds(j, tokens, stride=8), :]
        out_ref[j] = (silu(rows) * scale).astype(BF16)


def pack_q(queries, decay):
    tokens, heads, dim = queries.shape
    return pl.pallas_call(
        pack_q_kernel,
        grid=(heads // 8,),
        in_specs=[
            pl.BlockSpec((tokens, heads), lambda g: (0, 0)),
            pl.BlockSpec((tokens, 8, dim), lambda g: (0, g, 0)),
        ],
        out_specs=pl.BlockSpec((8, tokens, dim), lambda g: (g, 0, 0)),
        out_shape=jax.ShapeDtypeStruct((heads, tokens, dim), BF16),
        scratch_shapes=[pltpu.VMEM((tokens * 8, dim), F32)],
        compiler_params=pltpu.CompilerParams(vmem_limit_bytes=LIMIT),
        name="pack_q",
    )(decay, queries)


def states_kernel(per_block, kv_ref, prefix_ref, total_ref, factor_ref, enter_ref, reach_ref):
    sources, rows, dim = kv_ref.shape
    tokens = (rows - EXTRA) // 2
    blocks = sources // per_block
    length = per_block * tokens
    tail = kv_ref[:, 2 * tokens : rows, :].astype(F32)
    totals = jnp.sum(tail, axis=1)
    parts = three_parts(totals)
    at, of = iota((sources, sources), 0), iota((sources, sources), 1)
    same = at // per_block == of // per_block

    def mask(keep):
        return keep.astype(F32).astype(BF16)

    before = dot_parts(mask(same & (of < at)), parts)
    after = dot_parts(mask(same & (of > at)), parts)
    enter_ref[...] = jnp.exp(before)
    to_block_end = jnp.exp(after)
    block_at, source_of = iota((blocks, sources), 0), iota((blocks, sources), 1) // per_block
    block_total = dot_parts(mask(block_at == source_of), parts)
    block_before = dot_parts(mask(block_at > source_of), parts)
    reach_ref[...] = jnp.exp(block_before)
    in_lanes = jnp.transpose(totals)[0:blocks, :]
    picked = jnp.where(block_at == source_of, in_lanes, 0.0)
    member, position = iota((sources, length), 0), iota((sources, length), 1)
    up_to = mask(lax.rem(member, per_block) <= position // tokens)
    through = sum(jnp.dot(part, up_to, preferred_element_type=F32) for part in three_parts(picked))
    source_row = iota((per_block, length), 0)
    source_col = iota((per_block, length), 1) // tokens
    repeats = length // dim
    state = jnp.zeros((dim, dim), F32)
    for b in range(blocks):
        here = slice(b * per_block, (b + 1) * per_block)
        start = jnp.concatenate([before[here]] * repeats, axis=1)
        factor_ref[b] = jnp.where(
            source_col <= source_row, jnp.exp(start - through[b : b + 1, :]), 0.0
        )
        prefix_ref[b] = state
        keys = kv_ref[here, 0:tokens, :].astype(F32) * to_block_end[here][:, None, :]
        values = kv_ref[here, tokens : 2 * tokens, :].reshape(length, dim)
        own = lax.dot_general(
            keys.astype(BF16).reshape(length, dim), values, (((0,), (0,)), ((), ())),
            preferred_element_type=F32,
        )
        state = jnp.exp(block_total[b : b + 1, :]) * state + own
    total_ref[0:dim, :] = state
    total_ref[dim : dim + 8, :] = jnp.broadcast_to(
        jnp.sum(block_total, axis=0, keepdims=True), (8, dim)
    )


def states(kv, per_block):
    sources, rows, dim = kv.shape
    blocks, length = sources // per_block, per_block * (rows - EXTRA) // 2
    return pl.pallas_call(
        functools.partial(states_kernel, per_block),
        out_shape=(
            jax.ShapeDtypeStruct((blocks, dim, dim), F32),
            jax.ShapeDtypeStruct((dim + 8, dim), F32),
            jax.ShapeDtypeStruct((blocks, per_block, length), F32),
            jax.ShapeDtypeStruct((sources, dim), F32),
            jax.ShapeDtypeStruct((blocks, dim), F32),
        ),
        compiler_params=pltpu.CompilerParams(vmem_limit_bytes=LIMIT),
        name="states",
    )(kv)


def attend_kernel(query_ref, kv_ref, prefix_ref, factor_ref, enter_ref, reach_ref, incoming_ref, out_ref):
    sources, tokens, dim = query_ref.shape
    blocks = prefix_ref.shape[0]
    per_block = sources // blocks
    length = per_block * tokens
    step = 128
    causal = iota((step, step), 0) >= iota((step, step), 1)

    def spread(x):
        return jnp.concatenate(
            [jnp.broadcast_to(x[i : i + 1], (tokens, x.shape[1])) for i in range(per_block)], axis=0
        )

    def weights(b):
        here = slice(b * per_block, (b + 1) * per_block)
        query = query_ref[here].reshape(length, dim)
        key = kv_ref[here, 0:tokens, :].reshape(length, dim)
        factor = spread(factor_ref[b])
        tiles = []
        for low in range(0, length, step):
            high = low + step
            scores = lax.dot_general(
                query[low:high], key[0:high], (((1,), (1,)), ((), ())), preferred_element_type=F32
            )
            scores = scores * factor[low:high, 0:high]
            diagonal = jnp.where(causal, scores[:, low:high], 0.0)
            if low:
                diagonal = jnp.concatenate([scores[:, 0:low], diagonal], axis=1)
            tiles.append(diagonal.astype(BF16))
        return tiles

    def finish(b, tiles):
        here = slice(b * per_block, (b + 1) * per_block)
        query = query_ref[here].reshape(length, dim)
        value = kv_ref[here, tokens : 2 * tokens, :].reshape(length, dim)
        state = prefix_ref[b] + reach_ref[b : b + 1, :] * incoming_ref[...]
        inter = jnp.dot(query, state.astype(BF16), preferred_element_type=F32)
        enter = spread(enter_ref[here])
        for low in range(0, length, step):
            high = low + step
            intra = jnp.dot(tiles[low // step], value[0:high], preferred_element_type=F32)
            mixed = (intra + enter[low:high] * inter[low:high]).astype(BF16)
            for i in range(low // 16, high // 16):
                source, row = divmod(i * 16, tokens)
                piece = mixed[i * 16 - low : i * 16 - low + 16]
                out_ref[b * per_block + source, row : row + 16, :] = piece

    tiles = weights(0)
    for b in range(blocks):
        following = weights(b + 1) if b + 1 < blocks else None
        finish(b, tiles)
        tiles = following


def attend(query, kv, prefix, factor, enter, reach, incoming):
    return pl.pallas_call(
        attend_kernel,
        out_shape=jax.ShapeDtypeStruct(query.shape, BF16),
        compiler_params=pltpu.CompilerParams(vmem_limit_bytes=LIMIT),
        name="attend",
    )(query, kv, prefix, factor, enter, reach, incoming)


def norm_kernel(parts, mixed_ref, gain_ref, out_hbm, rows, out, out_sem):
    heads, tokens, dim = mixed_ref.shape
    squares = [jnp.zeros((tokens, dim), F32) for _ in range(4)]
    for h in range(heads):
        x = mixed_ref[h].astype(F32)
        squares[h % 4] = squares[h % 4] + x * x
    total = squares[0] + squares[1] + squares[2] + squares[3]
    mean = jnp.sum(total, axis=1, keepdims=True) * (1.0 / (heads * dim))
    scale = jnp.broadcast_to(lax.rsqrt(mean + 1e-06), (tokens, dim))
    size = tokens // parts

    def copy_out(p):
        here = pl.ds(p * size, size)
        return pltpu.make_async_copy(out.at[here], out_hbm.at[here], out_sem.at[p])

    for p in range(parts):
        first, last = p * size, (p + 1) * size
        for h in range(heads):
            x = mixed_ref[h, first:last, :].astype(F32) * scale[first:last] * gain_ref[h : h + 1, :]
            rows[pl.ds(first * heads + h, size, stride=heads), :] = x
        for t in range(first, last):
            out[t] = rows[t * heads : (t + 1) * heads, :].astype(BF16)
        copy_out(p).start()
    for p in range(parts):
        copy_out(p).wait()


def norm(mixed, gain):
    heads, tokens, dim = mixed.shape
    parts = 6
    return pl.pallas_call(
        functools.partial(norm_kernel, parts),
        out_specs=pl.BlockSpec(memory_space=pl.ANY),
        out_shape=jax.ShapeDtypeStruct((tokens, heads, dim), BF16),
        scratch_shapes=[
            pltpu.VMEM((tokens * heads, dim), F32),
            pltpu.VMEM((tokens, heads, dim), BF16),
            pltpu.SemaphoreType.DMA((parts,)),
        ],
        compiler_params=pltpu.CompilerParams(vmem_limit_bytes=LIMIT),
        name="norm",
    )(mixed, gain)


def incoming_state(own):
    dim = own.shape[1]
    segment = lax.axis_index("seg")
    count = lax.axis_size("seg")
    whole = own
    entering = jnp.zeros_like(own)

    def join(earlier, later):
        decay = jnp.exp(later[dim : dim + 1])
        return jnp.concatenate([decay * earlier[:dim] + later[:dim], earlier[dim:] + later[dim:]], axis=0)

    hop = 1
    while hop < count // 2:
        other = lax.ppermute(whole, "seg", [(i, i ^ hop) for i in range(count)])
        upper = (segment & hop) != 0
        entering = jnp.where(upper, join(other, entering), entering)
        whole = jnp.where(upper, join(other, whole), join(whole, other))
        hop *= 2
    half = count // 2
    other = lax.ppermute(whole, "seg", [(i, i + half) for i in range(half)])
    return jnp.exp(entering[dim : dim + 1]) * other[:dim] + entering[:dim]


def shards(queries, keys, values, decay_log, out_gain):
    per_block = lax.axis_size("head")
    group = ("sub", "head")
    kv = lax.all_to_all(pack_kv(keys, values, decay_log), group, 0, 0, tiled=True)
    query = pack_q(queries, decay_log)
    query = lax.all_to_all(query, group, 0, 0, tiled=True)
    prefix, total, factor, enter, reach = states(kv, per_block)
    incoming = incoming_state(total)
    mixed = attend(query, kv, prefix, factor, enter, reach, incoming)
    mixed = lax.all_to_all(mixed, group, 0, 0, tiled=True)
    return norm(mixed, out_gain)


def solution(mesh):
    devices = mesh.devices
    contexts, per_block = devices.shape
    heads = 64
    sub = heads // per_block
    split = Mesh(devices.reshape(contexts // sub, sub, per_block), ("seg", "sub", "head"))
    rows = ("seg", "sub", "head")
    return jax.shard_map(
        shards,
        mesh=split,
        in_specs=(P(rows, None, None), P(rows, None, None), P(rows, None, None), P(rows, None), P()),
        out_specs=P(rows, None, None),
        check_vma=False,
    )
```

```python
import functools

import jax
import jax.numpy as jnp
from jax import lax
from jax.experimental import pallas as pl
from jax.experimental.pallas import tpu as pltpu
from jax.sharding import Mesh
from jax.sharding import PartitionSpec as P

F32 = jnp.float32
BF16 = jnp.bfloat16
GROUP = 16
EXTRA = 8
LIMIT = 16 * 1024 * 1024
FULL = 60 * 1024 * 1024


def iota(shape, axis):
    return lax.broadcasted_iota(jnp.int32, shape, axis)


def silu(x):
    half = 0.5 * x
    return half + half * jnp.tanh(half)


def three_parts(x):
    high = x.astype(BF16)
    rest = x - high.astype(F32)
    middle = rest.astype(BF16)
    low = (rest - middle.astype(F32)).astype(BF16)
    return high, middle, low


def dot_parts(mask, parts):
    return sum(jnp.dot(mask, part, preferred_element_type=F32) for part in parts)


def cumulative(decay):
    tokens, heads = decay.shape
    tril = (iota((tokens, tokens), 0) >= iota((tokens, tokens), 1)).astype(F32).astype(BF16)
    running = jnp.dot(tril, decay, preferred_element_type=F32)
    return jnp.concatenate([running, jnp.zeros((tokens, 128 - heads), F32)], axis=1)


def group_lanes(x, head):
    return pltpu.roll(x, lax.rem(128 - head, 128), 1)


def pack_kv_kernel(
    decay_hbm, keys_hbm, values_hbm, out_hbm,
    decay, keys, values, key_rows, value_rows, to_end, totals, out, decay_sem, in_sem, out_sem,
):
    tokens, heads, _ = keys.shape
    groups = heads // GROUP

    def copies_in(g):
        columns = pl.ds(g * GROUP, GROUP)
        return [
            pltpu.make_async_copy(source.at[:, columns, :], target.at[:, columns, :], in_sem.at[i, g])
            for i, (source, target) in enumerate(((keys_hbm, keys), (values_hbm, values)))
        ]

    def copy_out(g):
        here = pl.ds(g * GROUP, GROUP)
        return pltpu.make_async_copy(out.at[here], out_hbm.at[here], out_sem.at[g])

    decay_copy = pltpu.make_async_copy(decay_hbm, decay, decay_sem)
    decay_copy.start()
    for g in range(groups):
        for copy in copies_in(g):
            copy.start()
    decay_copy.wait()
    running = cumulative(decay[...])
    to_end[...] = jnp.exp(running[tokens - 1 : tokens, :] - running)
    row = iota((EXTRA, 128), 0)
    total = jnp.broadcast_to(running[tokens - 1 : tokens, :], (EXTRA, 128))
    high, middle, low = (part.astype(F32) for part in three_parts(total))
    totals[...] = jnp.where(row == 0, high, jnp.where(row == 1, middle, jnp.where(row == 2, low, 0.0)))

    def one(g, carry):
        for copy in copies_in(g):
            copy.wait()
        columns = pl.ds(g * GROUP, GROUP)
        scales, ends = group_lanes(to_end[...], g * GROUP), group_lanes(totals[...], g * GROUP)
        key_rows[...] = keys[:, columns, :].astype(F32).reshape(tokens * GROUP, 128)
        value_rows[...] = values[:, columns, :].astype(F32).reshape(tokens * GROUP, 128)
        for j in range(GROUP):
            rows = pl.ds(j, tokens, stride=GROUP)
            head = g * GROUP + j
            scale = jnp.broadcast_to(scales[:, j : j + 1], (tokens, 128))
            out[head, 0:tokens, :] = (silu(key_rows[rows, :]) * scale).astype(BF16)
            out[head, tokens : 2 * tokens, :] = silu(value_rows[rows, :]).astype(BF16)
            end = jnp.broadcast_to(ends[:, j : j + 1], (EXTRA, 128))
            out[head, 2 * tokens : 2 * tokens + EXTRA, :] = end.astype(BF16)
        copy_out(g).start()
        return carry

    lax.fori_loop(0, groups, one, 0)
    for g in range(groups):
        copy_out(g).wait()


def pack_kv(keys, values, decay):
    tokens, heads, dim = keys.shape
    anywhere = pl.BlockSpec(memory_space=pl.ANY)
    packed = (heads, 2 * tokens + EXTRA, dim)
    return pl.pallas_call(
        pack_kv_kernel,
        in_specs=[anywhere] * 3,
        out_specs=anywhere,
        out_shape=jax.ShapeDtypeStruct(packed, BF16),
        scratch_shapes=[
            pltpu.VMEM(decay.shape, BF16),
            pltpu.VMEM(keys.shape, BF16),
            pltpu.VMEM(values.shape, BF16),
            pltpu.VMEM((tokens * GROUP, dim), F32),
            pltpu.VMEM((tokens * GROUP, dim), F32),
            pltpu.VMEM((tokens, 128), F32),
            pltpu.VMEM((EXTRA, 128), F32),
            pltpu.VMEM(packed, BF16),
            pltpu.SemaphoreType.DMA,
            pltpu.SemaphoreType.DMA((2, heads // GROUP)),
            pltpu.SemaphoreType.DMA((heads // GROUP,)),
        ],
        compiler_params=pltpu.CompilerParams(vmem_limit_bytes=FULL),
        name="pack_kv",
    )(decay, keys, values)


def pack_q_kernel(decay_ref, queries_ref, out_ref, query_rows):
    tokens = queries_ref.shape[0]
    running = group_lanes(cumulative(decay_ref[...]), 8 * pl.program_id(0))
    query_rows[...] = queries_ref[...].astype(F32).reshape(tokens * 8, 128)
    grown = jnp.exp(running)
    for j in range(8):
        scale = jnp.broadcast_to(grown[:, j : j + 1], (tokens, 128))
        rows = query_rows[pl.ds(j, tokens, stride=8), :]
        out_ref[j] = (silu(rows) * scale).astype(BF16)


def pack_q(queries, decay):
    tokens, heads, dim = queries.shape
    return pl.pallas_call(
        pack_q_kernel,
        grid=(heads // 8,),
        in_specs=[
            pl.BlockSpec((tokens, heads), lambda g: (0, 0)),
            pl.BlockSpec((tokens, 8, dim), lambda g: (0, g, 0)),
        ],
        out_specs=pl.BlockSpec((8, tokens, dim), lambda g: (g, 0, 0)),
        out_shape=jax.ShapeDtypeStruct((heads, tokens, dim), BF16),
        scratch_shapes=[pltpu.VMEM((tokens * 8, dim), F32)],
        compiler_params=pltpu.CompilerParams(vmem_limit_bytes=LIMIT),
        name="pack_q",
    )(decay, queries)


def states_kernel(per_block, kv_ref, prefix_ref, total_ref, factor_ref, enter_ref, reach_ref):
    sources, rows, dim = kv_ref.shape
    tokens = (rows - EXTRA) // 2
    blocks = sources // per_block
    length = per_block * tokens
    tail = kv_ref[:, 2 * tokens : rows, :].astype(F32)
    totals = jnp.sum(tail, axis=1)
    parts = three_parts(totals)
    at, of = iota((sources, sources), 0), iota((sources, sources), 1)
    same = at // per_block == of // per_block

    def mask(keep):
        return keep.astype(F32).astype(BF16)

    before = dot_parts(mask(same & (of < at)), parts)
    after = dot_parts(mask(same & (of > at)), parts)
    enter_ref[...] = jnp.exp(before)
    to_block_end = jnp.exp(after)
    block_at, source_of = iota((blocks, sources), 0), iota((blocks, sources), 1) // per_block
    block_total = dot_parts(mask(block_at == source_of), parts)
    block_before = dot_parts(mask(block_at > source_of), parts)
    reach_ref[...] = jnp.exp(block_before)
    in_lanes = jnp.transpose(totals)[0:blocks, :]
    picked = jnp.where(block_at == source_of, in_lanes, 0.0)
    member, position = iota((sources, length), 0), iota((sources, length), 1)
    up_to = mask(lax.rem(member, per_block) <= position // tokens)
    through = sum(jnp.dot(part, up_to, preferred_element_type=F32) for part in three_parts(picked))
    source_row = iota((per_block, length), 0)
    source_col = iota((per_block, length), 1) // tokens
    repeats = length // dim
    state = jnp.zeros((dim, dim), F32)
    for b in range(blocks):
        here = slice(b * per_block, (b + 1) * per_block)
        start = jnp.concatenate([before[here]] * repeats, axis=1)
        factor_ref[b] = jnp.where(
            source_col <= source_row, jnp.exp(start - through[b : b + 1, :]), 0.0
        )
        prefix_ref[b] = state
        keys = kv_ref[here, 0:tokens, :].astype(F32) * to_block_end[here][:, None, :]
        values = kv_ref[here, tokens : 2 * tokens, :].reshape(length, dim)
        own = lax.dot_general(
            keys.astype(BF16).reshape(length, dim), values, (((0,), (0,)), ((), ())),
            preferred_element_type=F32,
        )
        state = jnp.exp(block_total[b : b + 1, :]) * state + own
    total_ref[0:dim, :] = state
    decay = jnp.exp(jnp.sum(block_total, axis=0, keepdims=True))
    total_ref[dim : dim + EXTRA, :] = jnp.broadcast_to(decay, (EXTRA, dim))


def states(kv, per_block):
    sources, rows, dim = kv.shape
    blocks, length = sources // per_block, per_block * (rows - EXTRA) // 2
    return pl.pallas_call(
        functools.partial(states_kernel, per_block),
        out_shape=(
            jax.ShapeDtypeStruct((blocks, dim, dim), F32),
            jax.ShapeDtypeStruct((dim + EXTRA, dim), F32),
            jax.ShapeDtypeStruct((blocks, per_block, length), F32),
            jax.ShapeDtypeStruct((sources, dim), F32),
            jax.ShapeDtypeStruct((blocks, dim), F32),
        ),
        compiler_params=pltpu.CompilerParams(vmem_limit_bytes=LIMIT),
        name="states",
    )(kv)


def attend_kernel(query_ref, kv_ref, prefix_ref, factor_ref, enter_ref, reach_ref, incoming_ref, out_ref):
    sources, tokens, dim = query_ref.shape
    blocks = prefix_ref.shape[0]
    per_block = sources // blocks
    length = per_block * tokens
    step = 128
    causal = iota((step, step), 0) >= iota((step, step), 1)

    def spread(x):
        return jnp.concatenate(
            [jnp.broadcast_to(x[i : i + 1], (tokens, x.shape[1])) for i in range(per_block)], axis=0
        )

    def weights(b):
        here = slice(b * per_block, (b + 1) * per_block)
        query = query_ref[here].reshape(length, dim)
        key = kv_ref[here, 0:tokens, :].reshape(length, dim)
        factor = spread(factor_ref[b])
        tiles = []
        for low in range(0, length, step):
            high = low + step
            scores = lax.dot_general(
                query[low:high], key[0:high], (((1,), (1,)), ((), ())), preferred_element_type=F32
            )
            scores = scores * factor[low:high, 0:high]
            diagonal = jnp.where(causal, scores[:, low:high], 0.0)
            if low:
                diagonal = jnp.concatenate([scores[:, 0:low], diagonal], axis=1)
            tiles.append(diagonal.astype(BF16))
        return tiles

    def finish(b, tiles):
        here = slice(b * per_block, (b + 1) * per_block)
        query = query_ref[here].reshape(length, dim)
        value = kv_ref[here, tokens : 2 * tokens, :].reshape(length, dim)
        state = prefix_ref[b] + reach_ref[b : b + 1, :] * incoming_ref[...]
        inter = jnp.dot(query, state.astype(BF16), preferred_element_type=F32)
        enter = spread(enter_ref[here])
        for low in range(0, length, step):
            high = low + step
            intra = jnp.dot(tiles[low // step], value[0:high], preferred_element_type=F32)
            mixed = (intra + enter[low:high] * inter[low:high]).astype(BF16)
            for i in range(low // 16, high // 16):
                source, row = divmod(i * 16, tokens)
                piece = mixed[i * 16 - low : i * 16 - low + 16]
                out_ref[b * per_block + source, row : row + 16, :] = piece

    tiles = weights(0)
    for b in range(blocks):
        following = weights(b + 1) if b + 1 < blocks else None
        finish(b, tiles)
        tiles = following


def attend(query, kv, prefix, factor, enter, reach, incoming):
    return pl.pallas_call(
        attend_kernel,
        out_shape=jax.ShapeDtypeStruct(query.shape, BF16),
        compiler_params=pltpu.CompilerParams(vmem_limit_bytes=LIMIT),
        name="attend",
    )(query, kv, prefix, factor, enter, reach, incoming)


def norm_kernel(parts, mixed_ref, gain_ref, out_hbm, rows, out, out_sem):
    heads, tokens, dim = mixed_ref.shape
    squares = [jnp.zeros((tokens, dim), F32) for _ in range(4)]
    for h in range(heads):
        x = mixed_ref[h].astype(F32)
        squares[h % 4] = squares[h % 4] + x * x
    total = squares[0] + squares[1] + squares[2] + squares[3]
    mean = jnp.sum(total, axis=1, keepdims=True) * (1.0 / (heads * dim))
    scale = jnp.broadcast_to(lax.rsqrt(mean + 1e-06), (tokens, dim))
    size = tokens // parts

    def copy_out(p):
        here = pl.ds(p * size, size)
        return pltpu.make_async_copy(out.at[here], out_hbm.at[here], out_sem.at[p])

    for p in range(parts):
        first, last = p * size, (p + 1) * size
        for h in range(heads):
            x = mixed_ref[h, first:last, :].astype(F32) * scale[first:last] * gain_ref[h : h + 1, :]
            rows[pl.ds(first * heads + h, size, stride=heads), :] = x
        for t in range(first, last):
            out[t] = rows[t * heads : (t + 1) * heads, :].astype(BF16)
        copy_out(p).start()
    for p in range(parts):
        copy_out(p).wait()


def norm(mixed, gain):
    heads, tokens, dim = mixed.shape
    parts = 6
    return pl.pallas_call(
        functools.partial(norm_kernel, parts),
        out_specs=pl.BlockSpec(memory_space=pl.ANY),
        out_shape=jax.ShapeDtypeStruct((tokens, heads, dim), BF16),
        scratch_shapes=[
            pltpu.VMEM((tokens * heads, dim), F32),
            pltpu.VMEM((tokens, heads, dim), BF16),
            pltpu.SemaphoreType.DMA((parts,)),
        ],
        compiler_params=pltpu.CompilerParams(vmem_limit_bytes=LIMIT),
        name="norm",
    )(mixed, gain)


def received(rows):
    dim = rows.shape[1]
    rows = rows.astype(F32)
    return rows[:dim], rows[dim : dim + 1]


def incoming_state(own):
    dim = own.shape[1]
    segment = lax.axis_index("seg")
    count = lax.axis_size("seg")
    whole = own
    entering_state, entering_decay = jnp.zeros((dim, dim), F32), jnp.ones((1, dim), F32)
    hop = 1
    while hop < count // 2:
        mine = whole.astype(BF16)
        state, decay = received(lax.ppermute(mine, "seg", [(i, i ^ hop) for i in range(count)]))
        upper = ((segment & hop) != 0).astype(F32)
        lower = 1.0 - upper
        entering_state = (upper * entering_decay) * state + entering_state
        entering_decay = entering_decay * (upper * decay + lower)
        own_decay = whole[dim : dim + 1]
        joined = (upper * own_decay + lower) * state + (lower * decay + upper) * whole[:dim]
        whole = jnp.concatenate([joined, jnp.broadcast_to(decay * own_decay, (EXTRA, dim))], axis=0)
        hop *= 2
    half = count // 2
    state, _ = received(lax.ppermute(whole.astype(BF16), "seg", [(i, i + half) for i in range(half)]))
    return entering_decay * state + entering_state


def shards(queries, keys, values, decay_log, out_gain):
    per_block = lax.axis_size("head")
    group = ("sub", "head")
    kv = lax.all_to_all(pack_kv(keys, values, decay_log), group, 0, 0, tiled=True)
    query = pack_q(queries, decay_log)
    query = lax.all_to_all(query, group, 0, 0, tiled=True)
    prefix, total, factor, enter, reach = states(kv, per_block)
    incoming = incoming_state(total)
    mixed = attend(query, kv, prefix, factor, enter, reach, incoming)
    mixed = lax.all_to_all(mixed, group, 0, 0, tiled=True)
    return norm(mixed, out_gain)


def solution(mesh):
    devices = mesh.devices
    contexts, per_block = devices.shape
    heads = 64
    sub = heads // per_block
    split = Mesh(devices.reshape(contexts // sub, sub, per_block), ("seg", "sub", "head"))
    rows = ("seg", "sub", "head")
    return jax.shard_map(
        shards,
        mesh=split,
        in_specs=(P(rows, None, None), P(rows, None, None), P(rows, None, None), P(rows, None), P()),
        out_specs=P(rows, None, None),
        check_vma=False,
    )
```

```python
import functools

import jax
import jax.numpy as jnp
from jax import lax
from jax.experimental import pallas as pl
from jax.experimental.pallas import tpu as pltpu
from jax.sharding import Mesh
from jax.sharding import PartitionSpec as P

F32 = jnp.float32
BF16 = jnp.bfloat16
GROUP = 16
EXTRA = 8
LIMIT = 16 * 1024 * 1024
FULL = 60 * 1024 * 1024


def iota(shape, axis):
    return lax.broadcasted_iota(jnp.int32, shape, axis)


def silu(x):
    half = 0.5 * x
    return half + half * jnp.tanh(half)


def three_parts(x):
    high = x.astype(BF16)
    rest = x - high.astype(F32)
    middle = rest.astype(BF16)
    low = (rest - middle.astype(F32)).astype(BF16)
    return high, middle, low


def dot_parts(mask, parts):
    return sum(jnp.dot(mask, part, preferred_element_type=F32) for part in parts)


def cumulative(decay):
    tokens, heads = decay.shape
    tril = (iota((tokens, tokens), 0) >= iota((tokens, tokens), 1)).astype(F32).astype(BF16)
    running = jnp.dot(tril, decay, preferred_element_type=F32)
    return jnp.concatenate([running, jnp.zeros((tokens, 128 - heads), F32)], axis=1)


def group_lanes(x, head):
    return pltpu.roll(x, lax.rem(128 - head, 128), 1)


def pack_kv_kernel(
    decay_hbm, keys_hbm, values_hbm, out_hbm,
    decay, keys, values, key_rows, value_rows, to_end, totals, out, decay_sem, in_sem, out_sem,
):
    tokens, heads, _ = keys.shape
    groups = heads // GROUP

    def copies_in(g):
        columns = pl.ds(g * GROUP, GROUP)
        return [
            pltpu.make_async_copy(source.at[:, columns, :], target.at[:, columns, :], in_sem.at[i, g])
            for i, (source, target) in enumerate(((keys_hbm, keys), (values_hbm, values)))
        ]

    def copy_out(g):
        here = pl.ds(g * GROUP, GROUP)
        return pltpu.make_async_copy(out.at[here], out_hbm.at[here], out_sem.at[g])

    decay_copy = pltpu.make_async_copy(decay_hbm, decay, decay_sem)
    decay_copy.start()
    for g in range(groups):
        for copy in copies_in(g):
            copy.start()
    decay_copy.wait()
    running = cumulative(decay[...])
    to_end[...] = jnp.exp(running[tokens - 1 : tokens, :] - running)
    row = iota((EXTRA, 128), 0)
    total = jnp.broadcast_to(running[tokens - 1 : tokens, :], (EXTRA, 128))
    high, middle, low = (part.astype(F32) for part in three_parts(total))
    totals[...] = jnp.where(row == 0, high, jnp.where(row == 1, middle, jnp.where(row == 2, low, 0.0)))

    def one(g, carry):
        for copy in copies_in(g):
            copy.wait()
        columns = pl.ds(g * GROUP, GROUP)
        scales, ends = group_lanes(to_end[...], g * GROUP), group_lanes(totals[...], g * GROUP)
        key_rows[...] = keys[:, columns, :].astype(F32).reshape(tokens * GROUP, 128)
        value_rows[...] = values[:, columns, :].astype(F32).reshape(tokens * GROUP, 128)
        for j in range(GROUP):
            rows = pl.ds(j, tokens, stride=GROUP)
            head = g * GROUP + j
            scale = jnp.broadcast_to(scales[:, j : j + 1], (tokens, 128))
            out[head, 0:tokens, :] = (silu(key_rows[rows, :]) * scale).astype(BF16)
            out[head, tokens : 2 * tokens, :] = silu(value_rows[rows, :]).astype(BF16)
            end = jnp.broadcast_to(ends[:, j : j + 1], (EXTRA, 128))
            out[head, 2 * tokens : 2 * tokens + EXTRA, :] = end.astype(BF16)
        copy_out(g).start()
        return carry

    lax.fori_loop(0, groups, one, 0)
    for g in range(groups):
        copy_out(g).wait()


def pack_kv(keys, values, decay):
    tokens, heads, dim = keys.shape
    anywhere = pl.BlockSpec(memory_space=pl.ANY)
    packed = (heads, 2 * tokens + EXTRA, dim)
    return pl.pallas_call(
        pack_kv_kernel,
        in_specs=[anywhere] * 3,
        out_specs=anywhere,
        out_shape=jax.ShapeDtypeStruct(packed, BF16),
        scratch_shapes=[
            pltpu.VMEM(decay.shape, BF16),
            pltpu.VMEM(keys.shape, BF16),
            pltpu.VMEM(values.shape, BF16),
            pltpu.VMEM((tokens * GROUP, dim), F32),
            pltpu.VMEM((tokens * GROUP, dim), F32),
            pltpu.VMEM((tokens, 128), F32),
            pltpu.VMEM((EXTRA, 128), F32),
            pltpu.VMEM(packed, BF16),
            pltpu.SemaphoreType.DMA,
            pltpu.SemaphoreType.DMA((2, heads // GROUP)),
            pltpu.SemaphoreType.DMA((heads // GROUP,)),
        ],
        compiler_params=pltpu.CompilerParams(vmem_limit_bytes=FULL),
        name="pack_kv",
    )(decay, keys, values)


def pack_q_kernel(decay_ref, queries_ref, out_ref, query_rows):
    tokens = queries_ref.shape[0]
    running = group_lanes(cumulative(decay_ref[...]), 8 * pl.program_id(0))
    query_rows[...] = queries_ref[...].astype(F32).reshape(tokens * 8, 128)
    grown = jnp.exp(running)
    for j in range(8):
        scale = jnp.broadcast_to(grown[:, j : j + 1], (tokens, 128))
        rows = query_rows[pl.ds(j, tokens, stride=8), :]
        out_ref[j] = (silu(rows) * scale).astype(BF16)


def pack_q(queries, decay):
    tokens, heads, dim = queries.shape
    return pl.pallas_call(
        pack_q_kernel,
        grid=(heads // 8,),
        in_specs=[
            pl.BlockSpec((tokens, heads), lambda g: (0, 0)),
            pl.BlockSpec((tokens, 8, dim), lambda g: (0, g, 0)),
        ],
        out_specs=pl.BlockSpec((8, tokens, dim), lambda g: (g, 0, 0)),
        out_shape=jax.ShapeDtypeStruct((heads, tokens, dim), BF16),
        scratch_shapes=[pltpu.VMEM((tokens * 8, dim), F32)],
        compiler_params=pltpu.CompilerParams(vmem_limit_bytes=LIMIT),
        name="pack_q",
    )(decay, queries)


def block_of(ref, b, blocks, first, last):
    return jnp.concatenate([ref[i, first:last, :] for i in range(b, ref.shape[0], blocks)], axis=0)


def states_kernel(per_block, kv_ref, prefix_ref, total_ref, factor_ref, enter_ref, reach_ref):
    sources, rows, dim = kv_ref.shape
    tokens = (rows - EXTRA) // 2
    blocks = sources // per_block
    length = per_block * tokens
    tail = kv_ref[:, 2 * tokens : rows, :].astype(F32)
    totals = jnp.sum(tail, axis=1)
    parts = three_parts(totals)
    at, of = iota((sources, sources), 0), iota((sources, sources), 1)
    same = at // per_block == of % blocks
    at_place, of_place = at % per_block, of // blocks

    def mask(keep):
        return keep.astype(F32).astype(BF16)

    before = dot_parts(mask(same & (of_place < at_place)), parts)
    after = dot_parts(mask(same & (of_place > at_place)), parts)
    enter_ref[...] = jnp.exp(before)
    to_block_end = jnp.exp(after)
    block_at, source_of = iota((blocks, sources), 0), iota((blocks, sources), 1) % blocks
    block_total = dot_parts(mask(block_at == source_of), parts)
    block_before = dot_parts(mask(block_at > source_of), parts)
    reach_ref[...] = jnp.exp(block_before)
    in_lanes = jnp.transpose(totals)[0:blocks, :]
    picked = jnp.where(block_at == source_of, in_lanes, 0.0)
    member, position = iota((sources, length), 0), iota((sources, length), 1)
    up_to = mask(member // blocks <= position // tokens)
    through = sum(jnp.dot(part, up_to, preferred_element_type=F32) for part in three_parts(picked))
    source_row = iota((per_block, length), 0)
    source_col = iota((per_block, length), 1) // tokens
    repeats = length // dim
    state = jnp.zeros((dim, dim), F32)
    for b in range(blocks):
        here = slice(b * per_block, (b + 1) * per_block)
        start = jnp.concatenate([before[here]] * repeats, axis=1)
        factor_ref[b] = jnp.where(
            source_col <= source_row, jnp.exp(start - through[b : b + 1, :]), 0.0
        )
        prefix_ref[b] = state
        keys = jnp.concatenate(
            [
                kv_ref[p * blocks + b, 0:tokens, :].astype(F32) * to_block_end[b * per_block + p][None]
                for p in range(per_block)
            ],
            axis=0,
        )
        own = lax.dot_general(
            keys.astype(BF16), block_of(kv_ref, b, blocks, tokens, 2 * tokens), (((0,), (0,)), ((), ())),
            preferred_element_type=F32,
        )
        state = jnp.exp(block_total[b : b + 1, :]) * state + own
    total_ref[0:dim, :] = state
    decay = jnp.exp(jnp.sum(block_total, axis=0, keepdims=True))
    total_ref[dim : dim + EXTRA, :] = jnp.broadcast_to(decay, (EXTRA, dim))


def states(kv, per_block):
    sources, rows, dim = kv.shape
    blocks, length = sources // per_block, per_block * (rows - EXTRA) // 2
    return pl.pallas_call(
        functools.partial(states_kernel, per_block),
        out_shape=(
            jax.ShapeDtypeStruct((blocks, dim, dim), F32),
            jax.ShapeDtypeStruct((dim + EXTRA, dim), F32),
            jax.ShapeDtypeStruct((blocks, per_block, length), F32),
            jax.ShapeDtypeStruct((sources, dim), F32),
            jax.ShapeDtypeStruct((blocks, dim), F32),
        ),
        compiler_params=pltpu.CompilerParams(vmem_limit_bytes=LIMIT),
        name="states",
    )(kv)


def attend_kernel(query_ref, kv_ref, prefix_ref, factor_ref, enter_ref, reach_ref, incoming_ref, out_ref):
    sources, tokens, dim = query_ref.shape
    blocks = prefix_ref.shape[0]
    per_block = sources // blocks
    length = per_block * tokens
    step = 128
    causal = iota((step, step), 0) >= iota((step, step), 1)

    def spread(x):
        return jnp.concatenate(
            [jnp.broadcast_to(x[i : i + 1], (tokens, x.shape[1])) for i in range(per_block)], axis=0
        )

    def weights(b):
        query = block_of(query_ref, b, blocks, 0, tokens)
        key = block_of(kv_ref, b, blocks, 0, tokens)
        factor = spread(factor_ref[b])
        tiles = []
        for low in range(0, length, step):
            high = low + step
            scores = lax.dot_general(
                query[low:high], key[0:high], (((1,), (1,)), ((), ())), preferred_element_type=F32
            )
            scores = scores * factor[low:high, 0:high]
            diagonal = jnp.where(causal, scores[:, low:high], 0.0)
            if low:
                diagonal = jnp.concatenate([scores[:, 0:low], diagonal], axis=1)
            tiles.append(diagonal.astype(BF16))
        return tiles

    def finish(b, tiles):
        here = slice(b * per_block, (b + 1) * per_block)
        query = block_of(query_ref, b, blocks, 0, tokens)
        value = block_of(kv_ref, b, blocks, tokens, 2 * tokens)
        state = prefix_ref[b] + reach_ref[b : b + 1, :] * incoming_ref[...]
        inter = jnp.dot(query, state.astype(BF16), preferred_element_type=F32)
        enter = spread(enter_ref[here])
        for low in range(0, length, step):
            high = low + step
            intra = jnp.dot(tiles[low // step], value[0:high], preferred_element_type=F32)
            mixed = (intra + enter[low:high] * inter[low:high]).astype(BF16)
            for i in range(low // 16, high // 16):
                source, row = divmod(i * 16, tokens)
                piece = mixed[i * 16 - low : i * 16 - low + 16]
                out_ref[source * blocks + b, row : row + 16, :] = piece

    tiles = weights(0)
    for b in range(blocks):
        following = weights(b + 1) if b + 1 < blocks else None
        finish(b, tiles)
        tiles = following


def attend(query, kv, prefix, factor, enter, reach, incoming):
    return pl.pallas_call(
        attend_kernel,
        out_shape=jax.ShapeDtypeStruct(query.shape, BF16),
        compiler_params=pltpu.CompilerParams(vmem_limit_bytes=LIMIT),
        name="attend",
    )(query, kv, prefix, factor, enter, reach, incoming)


def norm_kernel(parts, mixed_ref, gain_ref, out_hbm, rows, out, out_sem):
    heads, tokens, dim = mixed_ref.shape
    squares = [jnp.zeros((tokens, dim), F32) for _ in range(4)]
    for h in range(heads):
        x = mixed_ref[h].astype(F32)
        squares[h % 4] = squares[h % 4] + x * x
    total = squares[0] + squares[1] + squares[2] + squares[3]
    mean = jnp.sum(total, axis=1, keepdims=True) * (1.0 / (heads * dim))
    scale = jnp.broadcast_to(lax.rsqrt(mean + 1e-06), (tokens, dim))
    size = tokens // parts

    def copy_out(p):
        here = pl.ds(p * size, size)
        return pltpu.make_async_copy(out.at[here], out_hbm.at[here], out_sem.at[p])

    for p in range(parts):
        first, last = p * size, (p + 1) * size
        for h in range(heads):
            x = mixed_ref[h, first:last, :].astype(F32) * scale[first:last] * gain_ref[h : h + 1, :]
            rows[pl.ds(first * heads + h, size, stride=heads), :] = x
        for t in range(first, last):
            out[t] = rows[t * heads : (t + 1) * heads, :].astype(BF16)
        copy_out(p).start()
    for p in range(parts):
        copy_out(p).wait()


def norm(mixed, gain):
    heads, tokens, dim = mixed.shape
    parts = 6
    return pl.pallas_call(
        functools.partial(norm_kernel, parts),
        out_specs=pl.BlockSpec(memory_space=pl.ANY),
        out_shape=jax.ShapeDtypeStruct((tokens, heads, dim), BF16),
        scratch_shapes=[
            pltpu.VMEM((tokens * heads, dim), F32),
            pltpu.VMEM((tokens, heads, dim), BF16),
            pltpu.SemaphoreType.DMA((parts,)),
        ],
        compiler_params=pltpu.CompilerParams(vmem_limit_bytes=LIMIT),
        name="norm",
    )(mixed, gain)


def received(rows):
    dim = rows.shape[1]
    rows = rows.astype(F32)
    return rows[:dim], rows[dim : dim + 1]


def incoming_state(own):
    dim = own.shape[1]
    segment = lax.axis_index("seg")
    count = lax.axis_size("seg")
    whole = own
    entering_state, entering_decay = jnp.zeros((dim, dim), F32), jnp.ones((1, dim), F32)
    hop = 1
    while hop < count // 2:
        mine = whole.astype(BF16)
        state, decay = received(lax.ppermute(mine, "seg", [(i, i ^ hop) for i in range(count)]))
        upper = ((segment & hop) != 0).astype(F32)
        lower = 1.0 - upper
        entering_state = (upper * entering_decay) * state + entering_state
        entering_decay = entering_decay * (upper * decay + lower)
        own_decay = whole[dim : dim + 1]
        joined = (upper * own_decay + lower) * state + (lower * decay + upper) * whole[:dim]
        whole = jnp.concatenate([joined, jnp.broadcast_to(decay * own_decay, (EXTRA, dim))], axis=0)
        hop *= 2
    half = count // 2
    state, _ = received(lax.ppermute(
        whole.astype(BF16), "seg", [(i, half + (i + half // 2) % half) for i in range(half)]
    ))
    return entering_decay * state + entering_state


def shards(queries, keys, values, decay_log, out_gain):
    per_block = lax.axis_size("head")
    group = ("head", "sub")
    kv = lax.all_to_all(pack_kv(keys, values, decay_log), group, 0, 0, tiled=True)
    query = pack_q(queries, decay_log)
    query = lax.all_to_all(query, group, 0, 0, tiled=True)
    prefix, total, factor, enter, reach = states(kv, per_block)
    incoming = incoming_state(total)
    mixed = attend(query, kv, prefix, factor, enter, reach, incoming)
    mixed = lax.all_to_all(mixed, group, 0, 0, tiled=True)
    return norm(mixed, out_gain)


def solution(mesh):
    devices = mesh.devices
    contexts, per_block = devices.shape
    heads = 64
    sub = heads // per_block
    split = Mesh(devices.reshape(contexts // sub, sub, per_block), ("seg", "sub", "head"))
    rows = ("seg", "sub", "head")
    return jax.shard_map(
        shards,
        mesh=split,
        in_specs=(P(rows, None, None), P(rows, None, None), P(rows, None, None), P(rows, None), P()),
        out_specs=P(rows, None, None),
        check_vma=False,
    )
```

```python
import functools

import jax
import jax.numpy as jnp
from jax import lax
from jax.experimental import pallas as pl
from jax.experimental.pallas import tpu as pltpu
from jax.sharding import Mesh
from jax.sharding import PartitionSpec as P

F32 = jnp.float32
BF16 = jnp.bfloat16
GROUP = 16
EXTRA = 8
LIMIT = 16 * 1024 * 1024
FULL = 60 * 1024 * 1024


def iota(shape, axis):
    return lax.broadcasted_iota(jnp.int32, shape, axis)


def silu(x):
    half = 0.5 * x
    return half + half * jnp.tanh(half)


def three_parts(x):
    high = x.astype(BF16)
    rest = x - high.astype(F32)
    middle = rest.astype(BF16)
    low = (rest - middle.astype(F32)).astype(BF16)
    return high, middle, low


def dot_parts(mask, parts):
    return sum(jnp.dot(mask, part, preferred_element_type=F32) for part in parts)


def cumulative(decay):
    tokens, heads = decay.shape
    tril = (iota((tokens, tokens), 0) >= iota((tokens, tokens), 1)).astype(F32).astype(BF16)
    running = jnp.dot(tril, decay, preferred_element_type=F32)
    return jnp.concatenate([running, jnp.zeros((tokens, 128 - heads), F32)], axis=1)


def group_lanes(x, head):
    return pltpu.roll(x, lax.rem(128 - head, 128), 1)


def pack_kv_kernel(
    decay_hbm, keys_hbm, values_hbm, out_hbm,
    decay, keys, values, key_rows, value_rows, out, decay_sem, in_sem, out_sem, extra_sem,
):
    tokens, heads, _ = keys.shape
    groups = heads // GROUP

    def copy_in(i, g):
        source, target = ((values_hbm, values), (keys_hbm, keys))[i]
        columns = pl.ds(g * GROUP, GROUP)
        return pltpu.make_async_copy(source.at[:, columns, :], target.at[:, columns, :], in_sem.at[i, g])

    def copy_out(i, g):
        here, rows = pl.ds(g * GROUP, GROUP), pl.ds((1 - i) * tokens, tokens)
        return pltpu.make_async_copy(out.at[here, rows, :], out_hbm.at[here, rows, :], out_sem.at[i, g])

    extra = pl.ds(2 * tokens, EXTRA)
    extra_out = pltpu.make_async_copy(out.at[:, extra, :], out_hbm.at[:, extra, :], extra_sem)
    decay_copy = pltpu.make_async_copy(decay_hbm, decay, decay_sem)
    decay_copy.start()
    for i in range(2):
        for g in range(groups):
            copy_in(i, g).start()
    for g in range(groups):
        copy_in(0, g).wait()
        value_rows[...] = values[:, g * GROUP : (g + 1) * GROUP, :].astype(F32).reshape(tokens * GROUP, 128)
        for j in range(GROUP):
            value = value_rows[pl.ds(j, tokens, stride=GROUP), :]
            out[g * GROUP + j, tokens : 2 * tokens, :] = silu(value).astype(BF16)
        copy_out(0, g).start()
    decay_copy.wait()
    running = cumulative(decay[...])
    to_end = jnp.exp(running[tokens - 1 : tokens, :] - running)
    row = iota((EXTRA, 128), 0)
    total = jnp.broadcast_to(running[tokens - 1 : tokens, :], (EXTRA, 128))
    high, middle, low = (part.astype(F32) for part in three_parts(total))
    totals = jnp.where(row == 0, high, jnp.where(row == 1, middle, jnp.where(row == 2, low, 0.0)))
    for head in range(heads):
        end = jnp.broadcast_to(totals[:, head : head + 1], (EXTRA, 128))
        out[head, 2 * tokens : 2 * tokens + EXTRA, :] = end.astype(BF16)
    extra_out.start()
    for g in range(groups):
        copy_in(1, g).wait()
        key_rows[...] = keys[:, g * GROUP : (g + 1) * GROUP, :].astype(F32).reshape(tokens * GROUP, 128)
        for j in range(GROUP):
            head = g * GROUP + j
            scale = jnp.broadcast_to(to_end[:, head : head + 1], (tokens, 128))
            key = key_rows[pl.ds(j, tokens, stride=GROUP), :]
            out[head, 0:tokens, :] = (silu(key) * scale).astype(BF16)
        copy_out(1, g).start()
    for i in range(2):
        for g in range(groups):
            copy_out(i, g).wait()
    extra_out.wait()


def pack_kv(keys, values, decay):
    tokens, heads, dim = keys.shape
    anywhere = pl.BlockSpec(memory_space=pl.ANY)
    packed = (heads, 2 * tokens + EXTRA, dim)
    return pl.pallas_call(
        pack_kv_kernel,
        in_specs=[anywhere] * 3,
        out_specs=anywhere,
        out_shape=jax.ShapeDtypeStruct(packed, BF16),
        scratch_shapes=[
            pltpu.VMEM(decay.shape, BF16),
            pltpu.VMEM(keys.shape, BF16),
            pltpu.VMEM(values.shape, BF16),
            pltpu.VMEM((tokens * GROUP, dim), F32),
            pltpu.VMEM((tokens * GROUP, dim), F32),
            pltpu.VMEM(packed, BF16),
            pltpu.SemaphoreType.DMA,
            pltpu.SemaphoreType.DMA((2, heads // GROUP)),
            pltpu.SemaphoreType.DMA((2, heads // GROUP)),
            pltpu.SemaphoreType.DMA,
        ],
        compiler_params=pltpu.CompilerParams(vmem_limit_bytes=FULL),
        name="pack_kv",
    )(decay, keys, values)


def pack_q_kernel(decay_ref, queries_ref, out_ref, query_rows):
    tokens = queries_ref.shape[0]
    running = group_lanes(cumulative(decay_ref[...]), 8 * pl.program_id(0))
    query_rows[...] = queries_ref[...].astype(F32).reshape(tokens * 8, 128)
    grown = jnp.exp(running)
    for j in range(8):
        scale = jnp.broadcast_to(grown[:, j : j + 1], (tokens, 128))
        rows = query_rows[pl.ds(j, tokens, stride=8), :]
        out_ref[j] = (silu(rows) * scale).astype(BF16)


def pack_q(queries, decay):
    tokens, heads, dim = queries.shape
    return pl.pallas_call(
        pack_q_kernel,
        grid=(heads // 8,),
        in_specs=[
            pl.BlockSpec((tokens, heads), lambda g: (0, 0)),
            pl.BlockSpec((tokens, 8, dim), lambda g: (0, g, 0)),
        ],
        out_specs=pl.BlockSpec((8, tokens, dim), lambda g: (g, 0, 0)),
        out_shape=jax.ShapeDtypeStruct((heads, tokens, dim), BF16),
        scratch_shapes=[pltpu.VMEM((tokens * 8, dim), F32)],
        compiler_params=pltpu.CompilerParams(vmem_limit_bytes=LIMIT),
        name="pack_q",
    )(decay, queries)


def source_number(place, b, blocks):
    return place * blocks + b % 2 * (blocks // 2) + b // 2


def block_number(source, blocks):
    within = source % blocks
    return within % (blocks // 2) * 2 + within // (blocks // 2)


def block_of(ref, b, blocks, first, last):
    places = ref.shape[0] // blocks
    return jnp.concatenate([ref[source_number(p, b, blocks), first:last, :] for p in range(places)], axis=0)


def states_kernel(per_block, kv_ref, prefix_ref, total_ref, factor_ref, enter_ref, reach_ref):
    sources, rows, dim = kv_ref.shape
    tokens = (rows - EXTRA) // 2
    blocks = sources // per_block
    length = per_block * tokens
    tail = kv_ref[:, 2 * tokens : rows, :].astype(F32)
    totals = jnp.sum(tail, axis=1)
    parts = three_parts(totals)
    at, of = iota((sources, sources), 0), iota((sources, sources), 1)
    same = at // per_block == block_number(of, blocks)
    at_place, of_place = at % per_block, of // blocks

    def mask(keep):
        return keep.astype(F32).astype(BF16)

    before = dot_parts(mask(same & (of_place < at_place)), parts)
    after = dot_parts(mask(same & (of_place > at_place)), parts)
    enter_ref[...] = jnp.exp(before)
    to_block_end = jnp.exp(after)
    block_at, source_of = iota((blocks, sources), 0), block_number(iota((blocks, sources), 1), blocks)
    block_total = dot_parts(mask(block_at == source_of), parts)
    block_before = dot_parts(mask(block_at > source_of), parts)
    reach_ref[...] = jnp.exp(block_before)
    in_lanes = jnp.transpose(totals)[0:blocks, :]
    picked = jnp.where(block_at == source_of, in_lanes, 0.0)
    member, position = iota((sources, length), 0), iota((sources, length), 1)
    up_to = mask(member // blocks <= position // tokens)
    through = sum(jnp.dot(part, up_to, preferred_element_type=F32) for part in three_parts(picked))
    source_row = iota((per_block, length), 0)
    source_col = iota((per_block, length), 1) // tokens
    repeats = length // dim
    state = jnp.zeros((dim, dim), F32)
    for b in range(blocks):
        here = slice(b * per_block, (b + 1) * per_block)
        start = jnp.concatenate([before[here]] * repeats, axis=1)
        factor_ref[b] = jnp.where(
            source_col <= source_row, jnp.exp(start - through[b : b + 1, :]), 0.0
        )
        prefix_ref[b] = state
        keys = jnp.concatenate(
            [
                kv_ref[source_number(p, b, blocks), 0:tokens, :].astype(F32) * to_block_end[b * per_block + p][None]
                for p in range(per_block)
            ],
            axis=0,
        )
        own = lax.dot_general(
            keys.astype(BF16), block_of(kv_ref, b, blocks, tokens, 2 * tokens), (((0,), (0,)), ((), ())),
            preferred_element_type=F32,
        )
        state = jnp.exp(block_total[b : b + 1, :]) * state + own
    total_ref[0:dim, :] = state
    decay = jnp.exp(jnp.sum(block_total, axis=0, keepdims=True))
    total_ref[dim : dim + EXTRA, :] = jnp.broadcast_to(decay, (EXTRA, dim))


def states(kv, per_block):
    sources, rows, dim = kv.shape
    blocks, length = sources // per_block, per_block * (rows - EXTRA) // 2
    return pl.pallas_call(
        functools.partial(states_kernel, per_block),
        out_shape=(
            jax.ShapeDtypeStruct((blocks, dim, dim), F32),
            jax.ShapeDtypeStruct((dim + EXTRA, dim), F32),
            jax.ShapeDtypeStruct((blocks, per_block, length), F32),
            jax.ShapeDtypeStruct((sources, dim), F32),
            jax.ShapeDtypeStruct((blocks, dim), F32),
        ),
        compiler_params=pltpu.CompilerParams(vmem_limit_bytes=LIMIT),
        name="states",
    )(kv)


def attend_kernel(query_ref, kv_ref, prefix_ref, factor_ref, enter_ref, reach_ref, incoming_ref, out_ref):
    sources, tokens, dim = query_ref.shape
    blocks = prefix_ref.shape[0]
    per_block = sources // blocks
    length = per_block * tokens
    step = 128
    causal = iota((step, step), 0) >= iota((step, step), 1)

    def spread(x):
        return jnp.concatenate(
            [jnp.broadcast_to(x[i : i + 1], (tokens, x.shape[1])) for i in range(per_block)], axis=0
        )

    def weights(b):
        query = block_of(query_ref, b, blocks, 0, tokens)
        key = block_of(kv_ref, b, blocks, 0, tokens)
        factor = spread(factor_ref[b])
        tiles = []
        for low in range(0, length, step):
            high = low + step
            scores = lax.dot_general(
                query[low:high], key[0:high], (((1,), (1,)), ((), ())), preferred_element_type=F32
            )
            scores = scores * factor[low:high, 0:high]
            diagonal = jnp.where(causal, scores[:, low:high], 0.0)
            if low:
                diagonal = jnp.concatenate([scores[:, 0:low], diagonal], axis=1)
            tiles.append(diagonal.astype(BF16))
        return tiles

    def finish(b, tiles):
        here = slice(b * per_block, (b + 1) * per_block)
        query = block_of(query_ref, b, blocks, 0, tokens)
        value = block_of(kv_ref, b, blocks, tokens, 2 * tokens)
        state = prefix_ref[b] + reach_ref[b : b + 1, :] * incoming_ref[...]
        inter = jnp.dot(query, state.astype(BF16), preferred_element_type=F32)
        enter = spread(enter_ref[here])
        for low in range(0, length, step):
            high = low + step
            intra = jnp.dot(tiles[low // step], value[0:high], preferred_element_type=F32)
            mixed = (intra + enter[low:high] * inter[low:high]).astype(BF16)
            for i in range(low // 16, high // 16):
                source, row = divmod(i * 16, tokens)
                piece = mixed[i * 16 - low : i * 16 - low + 16]
                out_ref[source_number(source, b, blocks), row : row + 16, :] = piece

    tiles = weights(0)
    for b in range(blocks):
        following = weights(b + 1) if b + 1 < blocks else None
        finish(b, tiles)
        tiles = following


def attend(query, kv, prefix, factor, enter, reach, incoming):
    return pl.pallas_call(
        attend_kernel,
        out_shape=jax.ShapeDtypeStruct(query.shape, BF16),
        compiler_params=pltpu.CompilerParams(vmem_limit_bytes=LIMIT),
        name="attend",
    )(query, kv, prefix, factor, enter, reach, incoming)


def norm_kernel(parts, mixed_ref, gain_ref, out_hbm, rows, out, out_sem):
    heads, tokens, dim = mixed_ref.shape
    squares = [jnp.zeros((tokens, dim), F32) for _ in range(4)]
    for h in range(heads):
        x = mixed_ref[h].astype(F32)
        squares[h % 4] = squares[h % 4] + x * x
    total = squares[0] + squares[1] + squares[2] + squares[3]
    mean = jnp.sum(total, axis=1, keepdims=True) * (1.0 / (heads * dim))
    scale = jnp.broadcast_to(lax.rsqrt(mean + 1e-06), (tokens, dim))
    size = tokens // parts

    def copy_out(p):
        here = pl.ds(p * size, size)
        return pltpu.make_async_copy(out.at[here], out_hbm.at[here], out_sem.at[p])

    for p in range(parts):
        first, last = p * size, (p + 1) * size
        for h in range(heads):
            x = mixed_ref[h, first:last, :].astype(F32) * scale[first:last] * gain_ref[h : h + 1, :]
            rows[pl.ds(first * heads + h, size, stride=heads), :] = x
        for t in range(first, last):
            out[t] = rows[t * heads : (t + 1) * heads, :].astype(BF16)
        copy_out(p).start()
    for p in range(parts):
        copy_out(p).wait()


def norm(mixed, gain):
    heads, tokens, dim = mixed.shape
    parts = 6
    return pl.pallas_call(
        functools.partial(norm_kernel, parts),
        out_specs=pl.BlockSpec(memory_space=pl.ANY),
        out_shape=jax.ShapeDtypeStruct((tokens, heads, dim), BF16),
        scratch_shapes=[
            pltpu.VMEM((tokens * heads, dim), F32),
            pltpu.VMEM((tokens, heads, dim), BF16),
            pltpu.SemaphoreType.DMA((parts,)),
        ],
        compiler_params=pltpu.CompilerParams(vmem_limit_bytes=LIMIT),
        name="norm",
    )(mixed, gain)


def received(rows):
    dim = rows.shape[1]
    rows = rows.astype(F32)
    return rows[:dim], rows[dim : dim + 1]


def incoming_state(own):
    dim = own.shape[1]
    segment = lax.axis_index("seg")
    count = lax.axis_size("seg")
    whole = own
    entering_state, entering_decay = jnp.zeros((dim, dim), F32), jnp.ones((1, dim), F32)
    hop = 1
    while hop < count // 2:
        mine = whole.astype(BF16)
        state, decay = received(lax.ppermute(mine, "seg", [(i, i ^ hop) for i in range(count)]))
        upper = ((segment & hop) != 0).astype(F32)
        lower = 1.0 - upper
        entering_state = (upper * entering_decay) * state + entering_state
        entering_decay = entering_decay * (upper * decay + lower)
        own_decay = whole[dim : dim + 1]
        joined = (upper * own_decay + lower) * state + (lower * decay + upper) * whole[:dim]
        whole = jnp.concatenate([joined, jnp.broadcast_to(decay * own_decay, (EXTRA, dim))], axis=0)
        hop *= 2
    half = count // 2
    state, _ = received(lax.ppermute(
        whole.astype(BF16), "seg", [(i, half + (i + half // 2) % half) for i in range(half)]
    ))
    return entering_decay * state + entering_state


def shards(queries, keys, values, decay_log, out_gain):
    per_block = lax.axis_size("head")
    group = ("head", "core", "chip")
    kv = lax.all_to_all(pack_kv(keys, values, decay_log), group, 0, 0, tiled=True)
    query = pack_q(queries, decay_log)
    query = lax.all_to_all(query, group, 0, 0, tiled=True)
    prefix, total, factor, enter, reach = states(kv, per_block)
    incoming = incoming_state(total)
    mixed = attend(query, kv, prefix, factor, enter, reach, incoming)
    mixed = lax.all_to_all(mixed, group, 0, 0, tiled=True)
    return norm(mixed, out_gain)


def solution(mesh):
    devices = mesh.devices
    contexts, per_block = devices.shape
    heads = 64
    sub = heads // per_block
    rows = ("seg", "chip", "core", "head")
    split = Mesh(devices.reshape(contexts // sub, sub // 2, 2, per_block), rows)
    return jax.shard_map(
        shards,
        mesh=split,
        in_specs=(P(rows, None, None), P(rows, None, None), P(rows, None, None), P(rows, None), P()),
        out_specs=P(rows, None, None),
        check_vma=False,
    )
```

```python
import functools

import jax
import jax.numpy as jnp
from jax import lax
from jax.experimental import pallas as pl
from jax.experimental.pallas import tpu as pltpu
from jax.sharding import Mesh
from jax.sharding import PartitionSpec as P

F32 = jnp.float32
BF16 = jnp.bfloat16
GROUP = 16
EXTRA = 8
LIMIT = 16 * 1024 * 1024
FULL = 60 * 1024 * 1024


def iota(shape, axis):
    return lax.broadcasted_iota(jnp.int32, shape, axis)


def silu(x):
    half = 0.5 * x
    return half + half * jnp.tanh(half)


def three_parts(x):
    high = x.astype(BF16)
    rest = x - high.astype(F32)
    middle = rest.astype(BF16)
    low = (rest - middle.astype(F32)).astype(BF16)
    return high, middle, low


def dot_parts(mask, parts):
    return sum(jnp.dot(mask, part, preferred_element_type=F32) for part in parts)


def cumulative(decay):
    tokens, heads = decay.shape
    tril = (iota((tokens, tokens), 0) >= iota((tokens, tokens), 1)).astype(F32).astype(BF16)
    running = jnp.dot(tril, decay, preferred_element_type=F32)
    return jnp.concatenate([running, jnp.zeros((tokens, 128 - heads), F32)], axis=1)


def group_lanes(x, head):
    return pltpu.roll(x, lax.rem(128 - head, 128), 1)


def pack_kv_kernel(
    decay_hbm, keys_hbm, values_hbm, out_hbm,
    decay, keys, values, key_rows, value_rows, out, decay_sem, in_sem, out_sem, extra_sem,
):
    tokens, heads, _ = keys.shape
    groups = heads // GROUP

    def copy_in(i, g):
        source, target = ((values_hbm, values), (keys_hbm, keys))[i]
        columns = pl.ds(g * GROUP, GROUP)
        return pltpu.make_async_copy(source.at[:, columns, :], target.at[:, columns, :], in_sem.at[i, g])

    def copy_out(i, g):
        here, rows = pl.ds(g * GROUP, GROUP), pl.ds((1 - i) * tokens, tokens)
        return pltpu.make_async_copy(out.at[here, rows, :], out_hbm.at[here, rows, :], out_sem.at[i, g])

    extra = pl.ds(2 * tokens, EXTRA)
    extra_out = pltpu.make_async_copy(out.at[:, extra, :], out_hbm.at[:, extra, :], extra_sem)
    decay_copy = pltpu.make_async_copy(decay_hbm, decay, decay_sem)
    decay_copy.start()
    for i in range(2):
        for g in range(groups):
            copy_in(i, g).start()
    for g in range(groups):
        copy_in(0, g).wait()
        value_rows[...] = values[:, g * GROUP : (g + 1) * GROUP, :].astype(F32).reshape(tokens * GROUP, 128)
        for j in range(GROUP):
            value = value_rows[pl.ds(j, tokens, stride=GROUP), :]
            out[g * GROUP + j, tokens : 2 * tokens, :] = silu(value).astype(BF16)
        copy_out(0, g).start()
    decay_copy.wait()
    running = cumulative(decay[...])
    to_end = jnp.exp(running[tokens - 1 : tokens, :] - running)
    row = iota((EXTRA, 128), 0)
    total = jnp.broadcast_to(running[tokens - 1 : tokens, :], (EXTRA, 128))
    high, middle, low = (part.astype(F32) for part in three_parts(total))
    totals = jnp.where(row == 0, high, jnp.where(row == 1, middle, jnp.where(row == 2, low, 0.0)))
    for head in range(heads):
        end = jnp.broadcast_to(totals[:, head : head + 1], (EXTRA, 128))
        out[head, 2 * tokens : 2 * tokens + EXTRA, :] = end.astype(BF16)
    extra_out.start()
    for g in range(groups):
        copy_in(1, g).wait()
        key_rows[...] = keys[:, g * GROUP : (g + 1) * GROUP, :].astype(F32).reshape(tokens * GROUP, 128)
        for j in range(GROUP):
            head = g * GROUP + j
            scale = jnp.broadcast_to(to_end[:, head : head + 1], (tokens, 128))
            key = key_rows[pl.ds(j, tokens, stride=GROUP), :]
            out[head, 0:tokens, :] = (silu(key) * scale).astype(BF16)
        copy_out(1, g).start()
    for i in range(2):
        for g in range(groups):
            copy_out(i, g).wait()
    extra_out.wait()


def pack_kv(keys, values, decay):
    tokens, heads, dim = keys.shape
    anywhere = pl.BlockSpec(memory_space=pl.ANY)
    packed = (heads, 2 * tokens + EXTRA, dim)
    return pl.pallas_call(
        pack_kv_kernel,
        in_specs=[anywhere] * 3,
        out_specs=anywhere,
        out_shape=jax.ShapeDtypeStruct(packed, BF16),
        scratch_shapes=[
            pltpu.VMEM(decay.shape, BF16),
            pltpu.VMEM(keys.shape, BF16),
            pltpu.VMEM(values.shape, BF16),
            pltpu.VMEM((tokens * GROUP, dim), F32),
            pltpu.VMEM((tokens * GROUP, dim), F32),
            pltpu.VMEM(packed, BF16),
            pltpu.SemaphoreType.DMA,
            pltpu.SemaphoreType.DMA((2, heads // GROUP)),
            pltpu.SemaphoreType.DMA((2, heads // GROUP)),
            pltpu.SemaphoreType.DMA,
        ],
        compiler_params=pltpu.CompilerParams(vmem_limit_bytes=FULL),
        name="pack_kv",
    )(decay, keys, values)


def pack_q_kernel(decay_ref, queries_ref, out_ref, query_rows):
    tokens = queries_ref.shape[0]
    running = group_lanes(cumulative(decay_ref[...]), 8 * pl.program_id(0))
    query_rows[...] = queries_ref[...].astype(F32).reshape(tokens * 8, 128)
    grown = jnp.exp(running)
    for j in range(8):
        scale = jnp.broadcast_to(grown[:, j : j + 1], (tokens, 128))
        rows = query_rows[pl.ds(j, tokens, stride=8), :]
        out_ref[j] = (silu(rows) * scale).astype(BF16)


def pack_q(queries, decay):
    tokens, heads, dim = queries.shape
    return pl.pallas_call(
        pack_q_kernel,
        grid=(heads // 8,),
        in_specs=[
            pl.BlockSpec((tokens, heads), lambda g: (0, 0)),
            pl.BlockSpec((tokens, 8, dim), lambda g: (0, g, 0)),
        ],
        out_specs=pl.BlockSpec((8, tokens, dim), lambda g: (g, 0, 0)),
        out_shape=jax.ShapeDtypeStruct((heads, tokens, dim), BF16),
        scratch_shapes=[pltpu.VMEM((tokens * 8, dim), F32)],
        compiler_params=pltpu.CompilerParams(vmem_limit_bytes=LIMIT),
        name="pack_q",
    )(decay, queries)


def source_number(place, b, blocks):
    return place * blocks + b % 2 * (blocks // 2) + b // 2


def block_number(source, blocks):
    within = source % blocks
    return within % (blocks // 2) * 2 + within // (blocks // 2)


def block_of(ref, b, blocks, first, last):
    places = ref.shape[0] // blocks
    return jnp.concatenate([ref[source_number(p, b, blocks), first:last, :] for p in range(places)], axis=0)


def states_kernel(per_block, kv_ref, prefix_ref, total_ref, factor_ref, enter_ref, reach_ref):
    sources, rows, dim = kv_ref.shape
    tokens = (rows - EXTRA) // 2
    blocks = sources // per_block
    length = per_block * tokens
    tail = kv_ref[:, 2 * tokens : rows, :].astype(F32)
    totals = jnp.sum(tail, axis=1)
    parts = three_parts(totals)
    at, of = iota((sources, sources), 0), iota((sources, sources), 1)
    same = at // per_block == block_number(of, blocks)
    at_place, of_place = at % per_block, of // blocks

    def mask(keep):
        return keep.astype(F32).astype(BF16)

    before = dot_parts(mask(same & (of_place < at_place)), parts)
    after = dot_parts(mask(same & (of_place > at_place)), parts)
    enter_ref[...] = jnp.exp(before)
    to_block_end = jnp.exp(after)
    block_at, source_of = iota((blocks, sources), 0), block_number(iota((blocks, sources), 1), blocks)
    block_total = dot_parts(mask(block_at == source_of), parts)
    block_before = dot_parts(mask(block_at > source_of), parts)
    reach_ref[...] = jnp.exp(block_before)
    in_lanes = jnp.transpose(totals)[0:blocks, :]
    picked = jnp.where(block_at == source_of, in_lanes, 0.0)
    member, position = iota((sources, length), 0), iota((sources, length), 1)
    up_to = mask(member // blocks <= position // tokens)
    through = sum(jnp.dot(part, up_to, preferred_element_type=F32) for part in three_parts(picked))
    source_row = iota((per_block, length), 0)
    source_col = iota((per_block, length), 1) // tokens
    repeats = length // dim
    state = jnp.zeros((dim, dim), F32)
    for b in range(blocks):
        here = slice(b * per_block, (b + 1) * per_block)
        start = jnp.concatenate([before[here]] * repeats, axis=1)
        factor_ref[b] = jnp.where(
            source_col <= source_row, jnp.exp(start - through[b : b + 1, :]), 0.0
        )
        prefix_ref[b] = state
        keys = jnp.concatenate(
            [
                kv_ref[source_number(p, b, blocks), 0:tokens, :].astype(F32) * to_block_end[b * per_block + p][None]
                for p in range(per_block)
            ],
            axis=0,
        )
        own = lax.dot_general(
            keys.astype(BF16), block_of(kv_ref, b, blocks, tokens, 2 * tokens), (((0,), (0,)), ((), ())),
            preferred_element_type=F32,
        )
        state = jnp.exp(block_total[b : b + 1, :]) * state + own
    total_ref[0:dim, :] = state
    decay = jnp.exp(jnp.sum(block_total, axis=0, keepdims=True))
    total_ref[dim : dim + EXTRA, :] = jnp.broadcast_to(decay, (EXTRA, dim))


def states(kv, per_block):
    sources, rows, dim = kv.shape
    blocks, length = sources // per_block, per_block * (rows - EXTRA) // 2
    return pl.pallas_call(
        functools.partial(states_kernel, per_block),
        out_shape=(
            jax.ShapeDtypeStruct((blocks, dim, dim), F32),
            jax.ShapeDtypeStruct((dim + EXTRA, dim), F32),
            jax.ShapeDtypeStruct((blocks, per_block, length), F32),
            jax.ShapeDtypeStruct((sources, dim), F32),
            jax.ShapeDtypeStruct((blocks, dim), F32),
        ),
        compiler_params=pltpu.CompilerParams(vmem_limit_bytes=LIMIT),
        name="states",
    )(kv)


def attend_kernel(query_ref, kv_ref, prefix_ref, factor_ref, enter_ref, reach_ref, incoming_ref, out_ref):
    sources, tokens, dim = query_ref.shape
    blocks = prefix_ref.shape[0]
    per_block = sources // blocks
    length = per_block * tokens
    step = 128
    causal = iota((step, step), 0) >= iota((step, step), 1)

    def spread(x):
        return jnp.concatenate(
            [jnp.broadcast_to(x[i : i + 1], (tokens, x.shape[1])) for i in range(per_block)], axis=0
        )

    def weights(b):
        query = block_of(query_ref, b, blocks, 0, tokens)
        key = block_of(kv_ref, b, blocks, 0, tokens)
        factor = spread(factor_ref[b])
        tiles = []
        for low in range(0, length, step):
            high = low + step
            scores = lax.dot_general(
                query[low:high], key[0:high], (((1,), (1,)), ((), ())), preferred_element_type=F32
            )
            scores = scores * factor[low:high, 0:high]
            diagonal = jnp.where(causal, scores[:, low:high], 0.0)
            if low:
                diagonal = jnp.concatenate([scores[:, 0:low], diagonal], axis=1)
            tiles.append(diagonal.astype(BF16))
        return tiles

    def finish(b, tiles):
        here = slice(b * per_block, (b + 1) * per_block)
        query = block_of(query_ref, b, blocks, 0, tokens)
        value = block_of(kv_ref, b, blocks, tokens, 2 * tokens)
        state = prefix_ref[b] + reach_ref[b : b + 1, :] * incoming_ref[...]
        inter = jnp.dot(query, state.astype(BF16), preferred_element_type=F32)
        enter = spread(enter_ref[here])
        for low in range(0, length, step):
            high = low + step
            intra = jnp.dot(tiles[low // step], value[0:high], preferred_element_type=F32)
            mixed = (intra + enter[low:high] * inter[low:high]).astype(BF16)
            for i in range(low // 16, high // 16):
                source, row = divmod(i * 16, tokens)
                piece = mixed[i * 16 - low : i * 16 - low + 16]
                out_ref[source_number(source, b, blocks), row : row + 16, :] = piece

    tiles = weights(0)
    for b in range(blocks):
        following = weights(b + 1) if b + 1 < blocks else None
        finish(b, tiles)
        tiles = following


def attend(query, kv, prefix, factor, enter, reach, incoming):
    return pl.pallas_call(
        attend_kernel,
        out_shape=jax.ShapeDtypeStruct(query.shape, BF16),
        compiler_params=pltpu.CompilerParams(vmem_limit_bytes=LIMIT),
        name="attend",
    )(query, kv, prefix, factor, enter, reach, incoming)


def norm_kernel(parts, mixed_ref, gain_ref, out_hbm, rows, out, out_sem):
    heads, tokens, dim = mixed_ref.shape
    squares = [jnp.zeros((tokens, dim), F32) for _ in range(4)]
    for h in range(heads):
        x = mixed_ref[h].astype(F32)
        squares[h % 4] = squares[h % 4] + x * x
    total = squares[0] + squares[1] + squares[2] + squares[3]
    mean = jnp.sum(total, axis=1, keepdims=True) * (1.0 / (heads * dim))
    scale = jnp.broadcast_to(lax.rsqrt(mean + 1e-06), (tokens, dim))
    size = tokens // parts

    def copy_out(p):
        here = pl.ds(p * size, size)
        return pltpu.make_async_copy(out.at[here], out_hbm.at[here], out_sem.at[p])

    for p in range(parts):
        first, last = p * size, (p + 1) * size
        for h in range(heads):
            x = mixed_ref[h, first:last, :].astype(F32) * scale[first:last] * gain_ref[h : h + 1, :]
            rows[pl.ds(first * heads + h, size, stride=heads), :] = x
        for t in range(first, last):
            out[t] = rows[t * heads : (t + 1) * heads, :].astype(BF16)
        copy_out(p).start()
    for p in range(parts):
        copy_out(p).wait()


def norm(mixed, gain):
    heads, tokens, dim = mixed.shape
    parts = 6
    return pl.pallas_call(
        functools.partial(norm_kernel, parts),
        out_specs=pl.BlockSpec(memory_space=pl.ANY),
        out_shape=jax.ShapeDtypeStruct((tokens, heads, dim), BF16),
        scratch_shapes=[
            pltpu.VMEM((tokens * heads, dim), F32),
            pltpu.VMEM((tokens, heads, dim), BF16),
            pltpu.SemaphoreType.DMA((parts,)),
        ],
        compiler_params=pltpu.CompilerParams(vmem_limit_bytes=LIMIT),
        name="norm",
    )(mixed, gain)


def received(rows):
    dim = rows.shape[1]
    rows = rows.astype(F32)
    return rows[:dim], rows[dim : dim + 1]


def incoming_state(own):
    dim = own.shape[1]
    segment = lax.axis_index("seg")
    count = lax.axis_size("seg")
    half, quarter = count // 2, count // 4
    pairs = [(i, i ^ 1) for i in range(count)]
    upward = [(i, i + quarter) for i in range(count) if i % half < quarter]
    whole = own
    entering_state, entering_decay = jnp.zeros((dim, dim), F32), jnp.ones((1, dim), F32)
    for hop, moves in ((1, pairs), (quarter, upward)):
        state, decay = received(lax.ppermute(whole.astype(BF16), "seg", moves))
        upper = ((segment & hop) != 0).astype(F32)
        lower = 1.0 - upper
        entering_state = (upper * entering_decay) * state + entering_state
        entering_decay = entering_decay * (upper * decay + lower)
        own_decay = whole[dim : dim + 1]
        joined = (upper * own_decay + lower) * state + (lower * decay + upper) * whole[:dim]
        whole = jnp.concatenate([joined, jnp.broadcast_to(decay * own_decay, (EXTRA, dim))], axis=0)
    near = lax.ppermute(whole[:dim].astype(BF16), "seg", [(i, i + quarter) for i in range(quarter, half)])
    far = lax.ppermute(near, "seg", [(i, i + quarter) for i in range(half, half + quarter)])
    return entering_decay * (near.astype(F32) + far.astype(F32)) + entering_state


def shards(queries, keys, values, decay_log, out_gain):
    per_block = lax.axis_size("head")
    group = ("head", "core", "chip")
    kv = lax.all_to_all(pack_kv(keys, values, decay_log), group, 0, 0, tiled=True)
    query = pack_q(queries, decay_log)
    query = lax.all_to_all(query, group, 0, 0, tiled=True)
    prefix, total, factor, enter, reach = states(kv, per_block)
    incoming = incoming_state(total)
    mixed = attend(query, kv, prefix, factor, enter, reach, incoming)
    mixed = lax.all_to_all(mixed, group, 0, 0, tiled=True)
    return norm(mixed, out_gain)


def solution(mesh):
    devices = mesh.devices
    contexts, per_block = devices.shape
    heads = 64
    sub = heads // per_block
    rows = ("seg", "chip", "core", "head")
    split = Mesh(devices.reshape(contexts // sub, sub // 2, 2, per_block), rows)
    return jax.shard_map(
        shards,
        mesh=split,
        in_specs=(P(rows, None, None), P(rows, None, None), P(rows, None, None), P(rows, None), P()),
        out_specs=P(rows, None, None),
        check_vma=False,
    )
```

```python
import functools

import jax
import jax.numpy as jnp
from jax import lax
from jax.experimental import pallas as pl
from jax.experimental.pallas import tpu as pltpu
from jax.sharding import Mesh
from jax.sharding import PartitionSpec as P

F32 = jnp.float32
BF16 = jnp.bfloat16
GROUP = 16
EXTRA = 8
LIMIT = 16 * 1024 * 1024
FULL = 60 * 1024 * 1024


def iota(shape, axis):
    return lax.broadcasted_iota(jnp.int32, shape, axis)


def silu(x):
    half = 0.5 * x
    return half + half * jnp.tanh(half)


def three_parts(x):
    high = x.astype(BF16)
    rest = x - high.astype(F32)
    middle = rest.astype(BF16)
    low = (rest - middle.astype(F32)).astype(BF16)
    return high, middle, low


def dot_parts(mask, parts):
    return sum(jnp.dot(mask, part, preferred_element_type=F32) for part in parts)


def cumulative(decay):
    tokens, heads = decay.shape
    tril = (iota((tokens, tokens), 0) >= iota((tokens, tokens), 1)).astype(F32).astype(BF16)
    running = jnp.dot(tril, decay, preferred_element_type=F32)
    return jnp.concatenate([running, jnp.zeros((tokens, 128 - heads), F32)], axis=1)


def group_lanes(x, head):
    return pltpu.roll(x, lax.rem(128 - head, 128), 1)


def pack_kv_kernel(
    decay_hbm, keys_hbm, values_hbm, out_hbm,
    decay, keys, values, key_rows, value_rows, out, decay_sem, in_sem, out_sem, extra_sem,
):
    tokens, heads, _ = keys.shape
    groups = heads // GROUP

    def copy_in(i, g):
        source, target = ((values_hbm, values), (keys_hbm, keys))[i]
        columns = pl.ds(g * GROUP, GROUP)
        return pltpu.make_async_copy(source.at[:, columns, :], target.at[:, columns, :], in_sem.at[i, g])

    def copy_out(i, g):
        here, rows = pl.ds(g * GROUP, GROUP), pl.ds((1 - i) * tokens, tokens)
        return pltpu.make_async_copy(out.at[here, rows, :], out_hbm.at[here, rows, :], out_sem.at[i, g])

    extra = pl.ds(2 * tokens, EXTRA)
    extra_out = pltpu.make_async_copy(out.at[:, extra, :], out_hbm.at[:, extra, :], extra_sem)
    decay_copy = pltpu.make_async_copy(decay_hbm, decay, decay_sem)
    decay_copy.start()
    for i in range(2):
        for g in range(groups):
            copy_in(i, g).start()
    for g in range(groups):
        copy_in(0, g).wait()
        value_rows[...] = values[:, g * GROUP : (g + 1) * GROUP, :].astype(F32).reshape(tokens * GROUP, 128)
        for j in range(GROUP):
            value = value_rows[pl.ds(j, tokens, stride=GROUP), :]
            out[g * GROUP + j, tokens : 2 * tokens, :] = silu(value).astype(BF16)
        copy_out(0, g).start()
    decay_copy.wait()
    running = cumulative(decay[...])
    to_end = jnp.exp(running[tokens - 1 : tokens, :] - running)
    row = iota((EXTRA, 128), 0)
    total = jnp.broadcast_to(running[tokens - 1 : tokens, :], (EXTRA, 128))
    high, middle, low = (part.astype(F32) for part in three_parts(total))
    totals = jnp.where(row == 0, high, jnp.where(row == 1, middle, jnp.where(row == 2, low, 0.0)))
    for head in range(heads):
        end = jnp.broadcast_to(totals[:, head : head + 1], (EXTRA, 128))
        out[head, 2 * tokens : 2 * tokens + EXTRA, :] = end.astype(BF16)
    extra_out.start()
    for g in range(groups):
        copy_in(1, g).wait()
        key_rows[...] = keys[:, g * GROUP : (g + 1) * GROUP, :].astype(F32).reshape(tokens * GROUP, 128)
        for j in range(GROUP):
            head = g * GROUP + j
            scale = jnp.broadcast_to(to_end[:, head : head + 1], (tokens, 128))
            key = key_rows[pl.ds(j, tokens, stride=GROUP), :]
            out[head, 0:tokens, :] = (silu(key) * scale).astype(BF16)
        copy_out(1, g).start()
    for i in range(2):
        for g in range(groups):
            copy_out(i, g).wait()
    extra_out.wait()


def pack_kv(keys, values, decay):
    tokens, heads, dim = keys.shape
    anywhere = pl.BlockSpec(memory_space=pl.ANY)
    packed = (heads, 2 * tokens + EXTRA, dim)
    return pl.pallas_call(
        pack_kv_kernel,
        in_specs=[anywhere] * 3,
        out_specs=anywhere,
        out_shape=jax.ShapeDtypeStruct(packed, BF16),
        scratch_shapes=[
            pltpu.VMEM(decay.shape, BF16),
            pltpu.VMEM(keys.shape, BF16),
            pltpu.VMEM(values.shape, BF16),
            pltpu.VMEM((tokens * GROUP, dim), F32),
            pltpu.VMEM((tokens * GROUP, dim), F32),
            pltpu.VMEM(packed, BF16),
            pltpu.SemaphoreType.DMA,
            pltpu.SemaphoreType.DMA((2, heads // GROUP)),
            pltpu.SemaphoreType.DMA((2, heads // GROUP)),
            pltpu.SemaphoreType.DMA,
        ],
        compiler_params=pltpu.CompilerParams(vmem_limit_bytes=FULL),
        name="pack_kv",
    )(decay, keys, values)


def pack_q_kernel(decay_ref, queries_ref, out_ref, query_rows):
    tokens = queries_ref.shape[0]
    running = group_lanes(cumulative(decay_ref[...]), 8 * pl.program_id(0))
    query_rows[...] = queries_ref[...].astype(F32).reshape(tokens * 8, 128)
    grown = jnp.exp(running)
    for j in range(8):
        scale = jnp.broadcast_to(grown[:, j : j + 1], (tokens, 128))
        rows = query_rows[pl.ds(j, tokens, stride=8), :]
        out_ref[j] = (silu(rows) * scale).astype(BF16)


def pack_q(queries, decay):
    tokens, heads, dim = queries.shape
    return pl.pallas_call(
        pack_q_kernel,
        grid=(heads // 8,),
        in_specs=[
            pl.BlockSpec((tokens, heads), lambda g: (0, 0)),
            pl.BlockSpec((tokens, 8, dim), lambda g: (0, g, 0)),
        ],
        out_specs=pl.BlockSpec((8, tokens, dim), lambda g: (g, 0, 0)),
        out_shape=jax.ShapeDtypeStruct((heads, tokens, dim), BF16),
        scratch_shapes=[pltpu.VMEM((tokens * 8, dim), F32)],
        compiler_params=pltpu.CompilerParams(vmem_limit_bytes=LIMIT),
        name="pack_q",
    )(decay, queries)


def source_number(place, b, blocks):
    return place * blocks + b % 2 * (blocks // 2) + b // 2


def block_number(source, blocks):
    within = source % blocks
    return within % (blocks // 2) * 2 + within // (blocks // 2)


def block_of(ref, b, blocks, first, last):
    places = ref.shape[0] // blocks
    return jnp.concatenate([ref[source_number(p, b, blocks), first:last, :] for p in range(places)], axis=0)


def states_kernel(per_block, kv_ref, prefix_ref, total_ref, factor_ref, enter_ref, reach_ref):
    sources, rows, dim = kv_ref.shape
    tokens = (rows - EXTRA) // 2
    blocks = sources // per_block
    length = per_block * tokens
    tail = kv_ref[:, 2 * tokens : rows, :].astype(F32)
    totals = jnp.sum(tail, axis=1)
    parts = three_parts(totals)
    at, of = iota((sources, sources), 0), iota((sources, sources), 1)
    same = at // per_block == block_number(of, blocks)
    at_place, of_place = at % per_block, of // blocks

    def mask(keep):
        return keep.astype(F32).astype(BF16)

    before = dot_parts(mask(same & (of_place < at_place)), parts)
    after = dot_parts(mask(same & (of_place > at_place)), parts)
    enter_ref[...] = jnp.exp(before)
    to_block_end = jnp.exp(after)
    block_at, source_of = iota((blocks, sources), 0), block_number(iota((blocks, sources), 1), blocks)
    block_total = dot_parts(mask(block_at == source_of), parts)
    block_before = dot_parts(mask(block_at > source_of), parts)
    reach_ref[...] = jnp.exp(block_before)
    in_lanes = jnp.transpose(totals)[0:blocks, :]
    picked = jnp.where(block_at == source_of, in_lanes, 0.0)
    member, position = iota((sources, length), 0), iota((sources, length), 1)
    up_to = mask(member // blocks <= position // tokens)
    through = sum(jnp.dot(part, up_to, preferred_element_type=F32) for part in three_parts(picked))
    source_row = iota((per_block, length), 0)
    source_col = iota((per_block, length), 1) // tokens
    repeats = length // dim
    state = jnp.zeros((dim, dim), F32)
    for b in range(blocks):
        here = slice(b * per_block, (b + 1) * per_block)
        start = jnp.concatenate([before[here]] * repeats, axis=1)
        factor_ref[b] = jnp.where(
            source_col <= source_row, jnp.exp(start - through[b : b + 1, :]), 0.0
        )
        prefix_ref[b] = state
        keys = jnp.concatenate(
            [
                kv_ref[source_number(p, b, blocks), 0:tokens, :].astype(F32) * to_block_end[b * per_block + p][None]
                for p in range(per_block)
            ],
            axis=0,
        )
        own = lax.dot_general(
            keys.astype(BF16), block_of(kv_ref, b, blocks, tokens, 2 * tokens), (((0,), (0,)), ((), ())),
            preferred_element_type=F32,
        )
        state = jnp.exp(block_total[b : b + 1, :]) * state + own
    total_ref[0:dim, :] = state
    decay = jnp.exp(jnp.sum(block_total, axis=0, keepdims=True))
    total_ref[dim : dim + EXTRA, :] = jnp.broadcast_to(decay, (EXTRA, dim))


def states(kv, per_block):
    sources, rows, dim = kv.shape
    blocks, length = sources // per_block, per_block * (rows - EXTRA) // 2
    return pl.pallas_call(
        functools.partial(states_kernel, per_block),
        out_shape=(
            jax.ShapeDtypeStruct((blocks, dim, dim), F32),
            jax.ShapeDtypeStruct((dim + EXTRA, dim), F32),
            jax.ShapeDtypeStruct((blocks, per_block, length), F32),
            jax.ShapeDtypeStruct((sources, dim), F32),
            jax.ShapeDtypeStruct((blocks, dim), F32),
        ),
        compiler_params=pltpu.CompilerParams(vmem_limit_bytes=LIMIT),
        name="states",
    )(kv)


def attend_kernel(query_ref, kv_ref, prefix_ref, factor_ref, enter_ref, reach_ref, incoming_ref, out_ref):
    sources, tokens, dim = query_ref.shape
    blocks = prefix_ref.shape[0]
    per_block = sources // blocks
    length = per_block * tokens
    step = 128
    causal = iota((step, step), 0) >= iota((step, step), 1)

    def spread(x):
        return jnp.concatenate(
            [jnp.broadcast_to(x[i : i + 1], (tokens, x.shape[1])) for i in range(per_block)], axis=0
        )

    def weights(b):
        query = block_of(query_ref, b, blocks, 0, tokens)
        key = block_of(kv_ref, b, blocks, 0, tokens)
        factor = spread(factor_ref[b])
        tiles = []
        for low in range(0, length, step):
            high = low + step
            scores = lax.dot_general(
                query[low:high], key[0:high], (((1,), (1,)), ((), ())), preferred_element_type=F32
            )
            scores = scores * factor[low:high, 0:high]
            diagonal = jnp.where(causal, scores[:, low:high], 0.0)
            if low:
                diagonal = jnp.concatenate([scores[:, 0:low], diagonal], axis=1)
            tiles.append(diagonal.astype(BF16))
        return tiles

    def finish(b, tiles):
        here = slice(b * per_block, (b + 1) * per_block)
        query = block_of(query_ref, b, blocks, 0, tokens)
        value = block_of(kv_ref, b, blocks, tokens, 2 * tokens)
        state = prefix_ref[b] + reach_ref[b : b + 1, :] * incoming_ref[...]
        inter = jnp.dot(query, state.astype(BF16), preferred_element_type=F32)
        enter = spread(enter_ref[here])
        for low in range(0, length, step):
            high = low + step
            intra = jnp.dot(tiles[low // step], value[0:high], preferred_element_type=F32)
            mixed = (intra + enter[low:high] * inter[low:high]).astype(BF16)
            for i in range(low // 16, high // 16):
                source, row = divmod(i * 16, tokens)
                piece = mixed[i * 16 - low : i * 16 - low + 16]
                out_ref[source_number(source, b, blocks), row : row + 16, :] = piece

    tiles = weights(0)
    for b in range(blocks):
        following = weights(b + 1) if b + 1 < blocks else None
        finish(b, tiles)
        tiles = following


def attend(query, kv, prefix, factor, enter, reach, incoming):
    return pl.pallas_call(
        attend_kernel,
        out_shape=jax.ShapeDtypeStruct(query.shape, BF16),
        compiler_params=pltpu.CompilerParams(vmem_limit_bytes=LIMIT),
        name="attend",
    )(query, kv, prefix, factor, enter, reach, incoming)


def norm_kernel(parts, mixed_ref, gain_ref, out_hbm, rows, out, out_sem):
    heads, tokens, dim = mixed_ref.shape
    squares = [jnp.zeros((tokens, dim), F32) for _ in range(4)]
    for h in range(heads):
        x = mixed_ref[h].astype(F32)
        squares[h % 4] = squares[h % 4] + x * x
    total = squares[0] + squares[1] + squares[2] + squares[3]
    mean = jnp.sum(total, axis=1, keepdims=True) * (1.0 / (heads * dim))
    scale = jnp.broadcast_to(lax.rsqrt(mean + 1e-06), (tokens, dim))
    size = tokens // parts

    def copy_out(p):
        here = pl.ds(p * size, size)
        return pltpu.make_async_copy(out.at[here], out_hbm.at[here], out_sem.at[p])

    for p in range(parts):
        first, last = p * size, (p + 1) * size
        for h in range(heads):
            x = mixed_ref[h, first:last, :].astype(F32) * scale[first:last] * gain_ref[h : h + 1, :]
            rows[pl.ds(first * heads + h, size, stride=heads), :] = x
        for t in range(first, last):
            out[t] = rows[t * heads : (t + 1) * heads, :].astype(BF16)
        copy_out(p).start()
    for p in range(parts):
        copy_out(p).wait()


def norm(mixed, gain):
    heads, tokens, dim = mixed.shape
    parts = 6
    return pl.pallas_call(
        functools.partial(norm_kernel, parts),
        out_specs=pl.BlockSpec(memory_space=pl.ANY),
        out_shape=jax.ShapeDtypeStruct((tokens, heads, dim), BF16),
        scratch_shapes=[
            pltpu.VMEM((tokens * heads, dim), F32),
            pltpu.VMEM((tokens, heads, dim), BF16),
            pltpu.SemaphoreType.DMA((parts,)),
        ],
        compiler_params=pltpu.CompilerParams(vmem_limit_bytes=LIMIT),
        name="norm",
    )(mixed, gain)


def received(rows):
    dim = rows.shape[1]
    rows = rows.astype(F32)
    return rows[:dim], rows[dim : dim + 1]


def incoming_state(own):
    dim = own.shape[1]
    segment = lax.axis_index("seg")
    odd = (segment & 1).astype(F32)
    second = ((segment & 2) != 0).astype(F32)
    rows = dim + EXTRA
    state, decay = received(lax.ppermute(own.astype(BF16), "seg", [(i, i ^ 1) for i in range(8)]))
    entering_state, entering_decay = odd * state, odd * decay + (1.0 - odd)
    own_decay = own[dim : dim + 1]
    joined = (odd * own_decay + (1.0 - odd)) * state + ((1.0 - odd) * decay + odd) * own[:dim]
    pair = jnp.concatenate([joined, jnp.broadcast_to(decay * own_decay, (EXTRA, dim))], axis=0).astype(BF16)
    first = lax.ppermute(pair, "seg", [(0, 6), (1, 7), (2, 4), (3, 5)])
    both = lax.ppermute(
        jnp.concatenate([pair, first], axis=0), "seg", [(0, 2), (1, 3), (4, 6), (5, 7), (6, 4), (7, 5)]
    )
    mine, mine_decay = received(first)
    before, before_decay = received(both[:rows])
    theirs, theirs_decay = received(both[rows:])
    early = second * mine + (1.0 - second) * theirs
    late, late_decay = second * theirs + (1.0 - second) * mine, second * theirs_decay + (1.0 - second) * mine_decay
    state = late + late_decay * early
    state = second * before + (second * before_decay + (1.0 - second)) * state
    return entering_decay * state + entering_state


def shards(queries, keys, values, decay_log, out_gain):
    per_block = lax.axis_size("head")
    group = ("head", "core", "chip")
    kv = lax.all_to_all(pack_kv(keys, values, decay_log), group, 0, 0, tiled=True)
    query = pack_q(queries, decay_log)
    query = lax.all_to_all(query, group, 0, 0, tiled=True)
    prefix, total, factor, enter, reach = states(kv, per_block)
    incoming = incoming_state(total)
    mixed = attend(query, kv, prefix, factor, enter, reach, incoming)
    mixed = lax.all_to_all(mixed, group, 0, 0, tiled=True)
    return norm(mixed, out_gain)


def solution(mesh):
    devices = mesh.devices
    contexts, per_block = devices.shape
    heads = 64
    sub = heads // per_block
    rows = ("seg", "chip", "core", "head")
    split = Mesh(devices.reshape(contexts // sub, sub // 2, 2, per_block), rows)
    return jax.shard_map(
        shards,
        mesh=split,
        in_specs=(P(rows, None, None), P(rows, None, None), P(rows, None, None), P(rows, None), P()),
        out_specs=P(rows, None, None),
        check_vma=False,
    )
```

```python
import functools

import jax
import jax.numpy as jnp
from jax import lax
from jax.experimental import pallas as pl
from jax.experimental.pallas import tpu as pltpu
from jax.sharding import Mesh
from jax.sharding import PartitionSpec as P

F32 = jnp.float32
BF16 = jnp.bfloat16
GROUP = 16
EXTRA = 8
LIMIT = 16 * 1024 * 1024
FULL = 60 * 1024 * 1024


def iota(shape, axis):
    return lax.broadcasted_iota(jnp.int32, shape, axis)


def silu(x):
    half = 0.5 * x
    return half + half * jnp.tanh(half)


def three_parts(x):
    high = x.astype(BF16)
    rest = x - high.astype(F32)
    middle = rest.astype(BF16)
    low = (rest - middle.astype(F32)).astype(BF16)
    return high, middle, low


def dot_parts(mask, parts):
    return sum(jnp.dot(mask, part, preferred_element_type=F32) for part in parts)


def cumulative(decay):
    tokens, heads = decay.shape
    tril = (iota((tokens, tokens), 0) >= iota((tokens, tokens), 1)).astype(F32).astype(BF16)
    running = jnp.dot(tril, decay, preferred_element_type=F32)
    return jnp.concatenate([running, jnp.zeros((tokens, 128 - heads), F32)], axis=1)


def group_lanes(x, head):
    return pltpu.roll(x, lax.rem(128 - head, 128), 1)


def pack_kv_kernel(
    decay_hbm, keys_hbm, values_hbm, out_hbm,
    decay, keys, values, key_rows, value_rows, out, decay_sem, in_sem, out_sem, extra_sem,
):
    tokens, heads, _ = keys.shape
    groups = heads // GROUP

    def copy_in(i, g):
        source, target = ((values_hbm, values), (keys_hbm, keys))[i]
        columns = pl.ds(g * GROUP, GROUP)
        return pltpu.make_async_copy(source.at[:, columns, :], target.at[:, columns, :], in_sem.at[i, g])

    def copy_out(i, g):
        here, rows = pl.ds(g * GROUP, GROUP), pl.ds((1 - i) * tokens, tokens)
        return pltpu.make_async_copy(out.at[here, rows, :], out_hbm.at[here, rows, :], out_sem.at[i, g])

    extra = pl.ds(2 * tokens, EXTRA)
    extra_out = pltpu.make_async_copy(out.at[:, extra, :], out_hbm.at[:, extra, :], extra_sem)
    decay_copy = pltpu.make_async_copy(decay_hbm, decay, decay_sem)
    decay_copy.start()
    for i in range(2):
        for g in range(groups):
            copy_in(i, g).start()
    for g in range(groups):
        copy_in(0, g).wait()
        value_rows[...] = values[:, g * GROUP : (g + 1) * GROUP, :].astype(F32).reshape(tokens * GROUP, 128)
        for j in range(GROUP):
            value = value_rows[pl.ds(j, tokens, stride=GROUP), :]
            out[g * GROUP + j, tokens : 2 * tokens, :] = silu(value).astype(BF16)
        copy_out(0, g).start()
    decay_copy.wait()
    running = cumulative(decay[...])
    to_end = jnp.exp(running[tokens - 1 : tokens, :] - running)
    row = iota((EXTRA, 128), 0)
    total = jnp.broadcast_to(running[tokens - 1 : tokens, :], (EXTRA, 128))
    high, middle, low = (part.astype(F32) for part in three_parts(total))
    totals = jnp.where(row == 0, high, jnp.where(row == 1, middle, jnp.where(row == 2, low, 0.0)))
    for head in range(heads):
        end = jnp.broadcast_to(totals[:, head : head + 1], (EXTRA, 128))
        out[head, 2 * tokens : 2 * tokens + EXTRA, :] = end.astype(BF16)
    extra_out.start()
    for g in range(groups):
        copy_in(1, g).wait()
        key_rows[...] = keys[:, g * GROUP : (g + 1) * GROUP, :].astype(F32).reshape(tokens * GROUP, 128)
        for j in range(GROUP):
            head = g * GROUP + j
            scale = jnp.broadcast_to(to_end[:, head : head + 1], (tokens, 128))
            key = key_rows[pl.ds(j, tokens, stride=GROUP), :]
            out[head, 0:tokens, :] = (silu(key) * scale).astype(BF16)
        copy_out(1, g).start()
    for i in range(2):
        for g in range(groups):
            copy_out(i, g).wait()
    extra_out.wait()


def pack_kv(keys, values, decay):
    tokens, heads, dim = keys.shape
    anywhere = pl.BlockSpec(memory_space=pl.ANY)
    packed = (heads, 2 * tokens + EXTRA, dim)
    return pl.pallas_call(
        pack_kv_kernel,
        in_specs=[anywhere] * 3,
        out_specs=anywhere,
        out_shape=jax.ShapeDtypeStruct(packed, BF16),
        scratch_shapes=[
            pltpu.VMEM(decay.shape, BF16),
            pltpu.VMEM(keys.shape, BF16),
            pltpu.VMEM(values.shape, BF16),
            pltpu.VMEM((tokens * GROUP, dim), F32),
            pltpu.VMEM((tokens * GROUP, dim), F32),
            pltpu.VMEM(packed, BF16),
            pltpu.SemaphoreType.DMA,
            pltpu.SemaphoreType.DMA((2, heads // GROUP)),
            pltpu.SemaphoreType.DMA((2, heads // GROUP)),
            pltpu.SemaphoreType.DMA,
        ],
        compiler_params=pltpu.CompilerParams(vmem_limit_bytes=FULL),
        name="pack_kv",
    )(decay, keys, values)


def pack_q_kernel(decay_ref, queries_ref, out_ref, query_rows):
    tokens = queries_ref.shape[0]
    running = group_lanes(cumulative(decay_ref[...]), 8 * pl.program_id(0))
    query_rows[...] = queries_ref[...].astype(F32).reshape(tokens * 8, 128)
    grown = jnp.exp(running)
    for j in range(8):
        scale = jnp.broadcast_to(grown[:, j : j + 1], (tokens, 128))
        rows = query_rows[pl.ds(j, tokens, stride=8), :]
        out_ref[j] = (silu(rows) * scale).astype(BF16)


def pack_q(queries, decay):
    tokens, heads, dim = queries.shape
    return pl.pallas_call(
        pack_q_kernel,
        grid=(heads // 8,),
        in_specs=[
            pl.BlockSpec((tokens, heads), lambda g: (0, 0)),
            pl.BlockSpec((tokens, 8, dim), lambda g: (0, g, 0)),
        ],
        out_specs=pl.BlockSpec((8, tokens, dim), lambda g: (g, 0, 0)),
        out_shape=jax.ShapeDtypeStruct((heads, tokens, dim), BF16),
        scratch_shapes=[pltpu.VMEM((tokens * 8, dim), F32)],
        compiler_params=pltpu.CompilerParams(vmem_limit_bytes=LIMIT),
        name="pack_q",
    )(decay, queries)


def source_number(place, b, blocks):
    return place * blocks + b % 2 * (blocks // 2) + b // 2


def block_number(source, blocks):
    within = source % blocks
    return within % (blocks // 2) * 2 + within // (blocks // 2)


def block_of(ref, b, blocks, first, last):
    places = ref.shape[0] // blocks
    return jnp.concatenate([ref[source_number(p, b, blocks), first:last, :] for p in range(places)], axis=0)


def states_kernel(per_block, kv_ref, prefix_ref, total_ref, factor_ref, enter_ref, reach_ref):
    sources, rows, dim = kv_ref.shape
    tokens = (rows - EXTRA) // 2
    blocks = sources // per_block
    length = per_block * tokens
    tail = kv_ref[:, 2 * tokens : rows, :].astype(F32)
    totals = jnp.sum(tail, axis=1)
    parts = three_parts(totals)
    at, of = iota((sources, sources), 0), iota((sources, sources), 1)
    same = at // per_block == block_number(of, blocks)
    at_place, of_place = at % per_block, of // blocks

    def mask(keep):
        return keep.astype(F32).astype(BF16)

    before = dot_parts(mask(same & (of_place < at_place)), parts)
    after = dot_parts(mask(same & (of_place > at_place)), parts)
    enter_ref[...] = jnp.exp(before)
    to_block_end = jnp.exp(after)
    block_at, source_of = iota((blocks, sources), 0), block_number(iota((blocks, sources), 1), blocks)
    block_total = dot_parts(mask(block_at == source_of), parts)
    block_before = dot_parts(mask(block_at > source_of), parts)
    reach_ref[...] = jnp.exp(block_before)
    in_lanes = jnp.transpose(totals)[0:blocks, :]
    picked = jnp.where(block_at == source_of, in_lanes, 0.0)
    member, position = iota((sources, length), 0), iota((sources, length), 1)
    up_to = mask(member // blocks <= position // tokens)
    through = sum(jnp.dot(part, up_to, preferred_element_type=F32) for part in three_parts(picked))
    source_row = iota((per_block, length), 0)
    source_col = iota((per_block, length), 1) // tokens
    repeats = length // dim
    state = jnp.zeros((dim, dim), F32)
    for b in range(blocks):
        here = slice(b * per_block, (b + 1) * per_block)
        start = jnp.concatenate([before[here]] * repeats, axis=1)
        factor_ref[b] = jnp.where(
            source_col <= source_row, jnp.exp(start - through[b : b + 1, :]), 0.0
        )
        prefix_ref[b] = state
        keys = jnp.concatenate(
            [
                kv_ref[source_number(p, b, blocks), 0:tokens, :].astype(F32) * to_block_end[b * per_block + p][None]
                for p in range(per_block)
            ],
            axis=0,
        )
        own = lax.dot_general(
            keys.astype(BF16), block_of(kv_ref, b, blocks, tokens, 2 * tokens), (((0,), (0,)), ((), ())),
            preferred_element_type=F32,
        )
        state = jnp.exp(block_total[b : b + 1, :]) * state + own
    total_ref[0:dim, :] = state
    decay = jnp.exp(jnp.sum(block_total, axis=0, keepdims=True))
    total_ref[dim : dim + EXTRA, :] = jnp.broadcast_to(decay, (EXTRA, dim))


def states(kv, per_block):
    sources, rows, dim = kv.shape
    blocks, length = sources // per_block, per_block * (rows - EXTRA) // 2
    return pl.pallas_call(
        functools.partial(states_kernel, per_block),
        out_shape=(
            jax.ShapeDtypeStruct((blocks, dim, dim), F32),
            jax.ShapeDtypeStruct((dim + EXTRA, dim), F32),
            jax.ShapeDtypeStruct((blocks, per_block, length), F32),
            jax.ShapeDtypeStruct((sources, dim), F32),
            jax.ShapeDtypeStruct((blocks, dim), F32),
        ),
        compiler_params=pltpu.CompilerParams(vmem_limit_bytes=LIMIT),
        name="states",
    )(kv)


def attend_kernel(query_ref, kv_ref, prefix_ref, factor_ref, enter_ref, reach_ref, incoming_ref, out_ref):
    sources, tokens, dim = query_ref.shape
    blocks = prefix_ref.shape[0]
    per_block = sources // blocks
    length = per_block * tokens
    step = 128
    causal = iota((step, step), 0) >= iota((step, step), 1)

    def spread(x):
        return jnp.concatenate(
            [jnp.broadcast_to(x[i : i + 1], (tokens, x.shape[1])) for i in range(per_block)], axis=0
        )

    def weights(b):
        query = block_of(query_ref, b, blocks, 0, tokens)
        key = block_of(kv_ref, b, blocks, 0, tokens)
        factor = spread(factor_ref[b])
        tiles = []
        for low in range(0, length, step):
            high = low + step
            scores = lax.dot_general(
                query[low:high], key[0:high], (((1,), (1,)), ((), ())), preferred_element_type=F32
            )
            scores = scores * factor[low:high, 0:high]
            diagonal = jnp.where(causal, scores[:, low:high], 0.0)
            if low:
                diagonal = jnp.concatenate([scores[:, 0:low], diagonal], axis=1)
            tiles.append(diagonal.astype(BF16))
        return tiles

    def finish(b, tiles):
        here = slice(b * per_block, (b + 1) * per_block)
        query = block_of(query_ref, b, blocks, 0, tokens)
        value = block_of(kv_ref, b, blocks, tokens, 2 * tokens)
        state = prefix_ref[b] + reach_ref[b : b + 1, :] * incoming_ref[...]
        inter = jnp.dot(query, state.astype(BF16), preferred_element_type=F32)
        enter = spread(enter_ref[here])
        for low in range(0, length, step):
            high = low + step
            intra = jnp.dot(tiles[low // step], value[0:high], preferred_element_type=F32)
            mixed = (intra + enter[low:high] * inter[low:high]).astype(BF16)
            for i in range(low // 16, high // 16):
                source, row = divmod(i * 16, tokens)
                piece = mixed[i * 16 - low : i * 16 - low + 16]
                out_ref[source_number(source, b, blocks), row : row + 16, :] = piece

    tiles = weights(0)
    for b in range(blocks):
        following = weights(b + 1) if b + 1 < blocks else None
        finish(b, tiles)
        tiles = following


def attend(query, kv, prefix, factor, enter, reach, incoming):
    return pl.pallas_call(
        attend_kernel,
        out_shape=jax.ShapeDtypeStruct(query.shape, BF16),
        compiler_params=pltpu.CompilerParams(vmem_limit_bytes=LIMIT),
        name="attend",
    )(query, kv, prefix, factor, enter, reach, incoming)


def norm_kernel(parts, mixed_ref, gain_ref, out_hbm, rows, out, out_sem):
    heads, tokens, dim = mixed_ref.shape
    squares = [jnp.zeros((tokens, dim), F32) for _ in range(4)]
    for h in range(heads):
        x = mixed_ref[h].astype(F32)
        squares[h % 4] = squares[h % 4] + x * x
    total = squares[0] + squares[1] + squares[2] + squares[3]
    mean = jnp.sum(total, axis=1, keepdims=True) * (1.0 / (heads * dim))
    scale = jnp.broadcast_to(lax.rsqrt(mean + 1e-06), (tokens, dim))
    size = tokens // parts

    def copy_out(p):
        here = pl.ds(p * size, size)
        return pltpu.make_async_copy(out.at[here], out_hbm.at[here], out_sem.at[p])

    for p in range(parts):
        first, last = p * size, (p + 1) * size
        for h in range(heads):
            x = mixed_ref[h, first:last, :].astype(F32) * scale[first:last] * gain_ref[h : h + 1, :]
            rows[pl.ds(first * heads + h, size, stride=heads), :] = x
        for t in range(first, last):
            out[t] = rows[t * heads : (t + 1) * heads, :].astype(BF16)
        copy_out(p).start()
    for p in range(parts):
        copy_out(p).wait()


def norm(mixed, gain):
    heads, tokens, dim = mixed.shape
    parts = 6
    return pl.pallas_call(
        functools.partial(norm_kernel, parts),
        out_specs=pl.BlockSpec(memory_space=pl.ANY),
        out_shape=jax.ShapeDtypeStruct((tokens, heads, dim), BF16),
        scratch_shapes=[
            pltpu.VMEM((tokens * heads, dim), F32),
            pltpu.VMEM((tokens, heads, dim), BF16),
            pltpu.SemaphoreType.DMA((parts,)),
        ],
        compiler_params=pltpu.CompilerParams(vmem_limit_bytes=LIMIT),
        name="norm",
    )(mixed, gain)


def received(rows):
    dim = rows.shape[1]
    rows = rows.astype(F32)
    return rows[:dim], rows[dim : dim + 1]


def incoming_state(own):
    dim = own.shape[1]
    segment = lax.axis_index("seg")
    odd = (segment & 1).astype(F32)
    second = ((segment & 2) != 0).astype(F32)
    rows = dim + EXTRA
    state, decay = received(lax.ppermute(own.astype(BF16), "seg", [(i, i ^ 1) for i in range(8)]))
    entering_state, entering_decay = odd * state, odd * decay + (1.0 - odd)
    own_decay = own[dim : dim + 1]
    joined = (odd * own_decay + (1.0 - odd)) * state + ((1.0 - odd) * decay + odd) * own[:dim]
    pair = jnp.concatenate([joined, jnp.broadcast_to(decay * own_decay, (EXTRA, dim))], axis=0).astype(BF16)
    first = lax.ppermute(pair, "seg", [(0, 4), (1, 5), (2, 6), (3, 7)])
    both = lax.ppermute(
        jnp.concatenate([pair, first], axis=0), "seg", [(0, 2), (1, 3), (4, 6), (5, 7), (6, 4), (7, 5)]
    )
    mine, mine_decay = received(first)
    before, before_decay = received(both[:rows])
    theirs, theirs_decay = received(both[rows:])
    early = second * theirs + (1.0 - second) * mine
    late, late_decay = second * mine + (1.0 - second) * theirs, second * mine_decay + (1.0 - second) * theirs_decay
    state = late + late_decay * early
    state = second * before + (second * before_decay + (1.0 - second)) * state
    return entering_decay * state + entering_state


def shards(queries, keys, values, decay_log, out_gain):
    per_block = lax.axis_size("head")
    group = ("head", "core", "chip")
    kv = lax.all_to_all(pack_kv(keys, values, decay_log), group, 0, 0, tiled=True)
    query = pack_q(queries, decay_log)
    query = lax.all_to_all(query, group, 0, 0, tiled=True)
    prefix, total, factor, enter, reach = states(kv, per_block)
    incoming = incoming_state(total)
    mixed = attend(query, kv, prefix, factor, enter, reach, incoming)
    mixed = lax.all_to_all(mixed, group, 0, 0, tiled=True)
    return norm(mixed, out_gain)


def solution(mesh):
    devices = mesh.devices
    contexts, per_block = devices.shape
    heads = 64
    sub = heads // per_block
    rows = ("seg", "chip", "core", "head")
    split = Mesh(devices.reshape(contexts // sub, sub // 2, 2, per_block), rows)
    return jax.shard_map(
        shards,
        mesh=split,
        in_specs=(P(rows, None, None), P(rows, None, None), P(rows, None, None), P(rows, None), P()),
        out_specs=P(rows, None, None),
        check_vma=False,
    )
```
